32 devices in a mesh: gz: 2 (over x), gx: 4 (over y, core), gy: 4 (over z).
Axes of the slice: x: 2, y: 2, z: 4, core: 2. Of those that a mesh axis runs over, the one named last changes fastest.
Arguments:
- sections: bfloat16 [2, 2560, 2560], P('gz', 'gy', 'gx'), may hold values from -440 to 440
- peaks: int32 [2, 2, 40, 40], P('gz', None, 'gy', 'gx'), may hold values from 0 to 127
- valid: int32 [2, 40, 40], P('gz', 'gy', 'gx'), may hold values 0 or 1
Outputs:
- fit: float32 [2, 6, 40, 40], P('gz', None, 'gy', 'gx')
The draws below stay inside these ranges and needn't reach their ends.
All inputs are finite; a program needn't handle non-finite values. Where the reference program divides by a largest or mean magnitude, that divisor is 1e-20 or more. No bound on the sum of `valid` on one device may be relied on, other than what follows from the above.
Results may differ from the reference program's by a relative error of at most 0.0089.
Values may be sent and summed in bfloat16 or wider, within the bound.
No kernel may reach another device: no remote copies, remote signals or barrier semaphores. Data moves between devices by JAX's collectives and lax.ppermute only.
A program may use at most 64 MiB of HBM per device.

```python
import math
import jax
import jax.numpy as jnp
from jax import lax

PATCH = 128
STRIDE = 64
WIN = 5
NSEC = 2
NY = 2560
NX = 2560
NPY = 40
NPX = 40


def draw_sections(key, part):
    first, second, third = jax.random.split(jax.random.fold_in(key, 11), 3)
    shape = (NSEC, NY, NX)
    base = jnp.clip(jax.random.normal(first, shape, jnp.float32), -4.0, 4.0)
    row_scale = jnp.exp(jax.random.uniform(second, (NSEC, NY, 1), jnp.float32, 0.0, math.log(10.0)))
    col_scale = jnp.exp(jax.random.uniform(third, (NSEC, 1, NX), jnp.float32, 0.0, math.log(10.0)))
    return (base * row_scale * col_scale).astype(jnp.bfloat16)


def place_ends(entries, stream_key, smallest, high):
    longest = entries.shape.index(max(entries.shape))
    spots = []
    for shift in (0, 1):
        where = [jax.random.randint(jax.random.fold_in(stream_key, axis), (), 0, length) for axis, length in enumerate(entries.shape)]
        where[longest] = (where[longest] + shift) % entries.shape[longest]
        spots.append(tuple(where))
    return entries.at[spots[0]].set(smallest).at[spots[1]].set(high)


def setup_inputs(seed: int = 0) -> dict:
    arg_keys = jax.random.split(jax.random.key(seed), 4)
    return {
        "sections": draw_sections(jax.random.fold_in(arg_keys[3], 71), 0),
        "peaks": place_ends(jax.random.randint(arg_keys[1], (NSEC, 2, NPY, NPX), 0, PATCH), jax.random.fold_in(arg_keys[1], 1), 0, PATCH - 1).astype(jnp.int32),
        "valid": place_ends((jax.random.randint(arg_keys[2], (NSEC, NPY, NPX), 0, 4) < 3).astype(jnp.int32), jax.random.fold_in(arg_keys[2], 1), 0, 1),
    }


def round_half(values):
    return lax.optimization_barrier(values.astype(jnp.bfloat16)).astype(jnp.float32)

def dft_tables(length):
    index = jnp.arange(length, dtype=jnp.int32)
    phase = (index[:, None] * index[None, :] % length).astype(jnp.float32) * (2.0 * math.pi / length)
    return (round_half(jnp.cos(phase)), round_half(jnp.sin(phase)))

def fit_basis(width):
    offsets = (jnp.arange(width, dtype=jnp.int32) - width // 2).astype(jnp.float32)
    ones = jnp.ones((width,), jnp.float32)
    square = offsets * offsets - jnp.mean(offsets * offsets)
    funcs = jnp.stack([ones[:, None] * ones[None, :], offsets[:, None] * ones[None, :], ones[:, None] * offsets[None, :], square[:, None] * ones[None, :], ones[:, None] * square[None, :], offsets[:, None] * offsets[None, :]], 0)
    return funcs / jnp.sqrt(lax.optimization_barrier(jnp.sum(funcs * funcs, axis=(1, 2), keepdims=True)))

def correlate_row(block, peak_row, valid_row):
    count = block.shape[0]
    length = block.shape[1]
    half = length // 2
    tiles = block.shape[2] // half - 1
    cosine, sine = dft_tables(length)
    columns = block.reshape(count, length, tiles + 1, half)
    patches = jnp.concatenate([columns[:, :, :-1], columns[:, :, 1:]], axis=3).astype(jnp.float32)
    energy = lax.optimization_barrier(jnp.mean(patches * patches, axis=(1, 3)))
    first_table = jnp.concatenate([cosine, -sine], 0)
    segment_one = round_half(jnp.einsum('cnjm,km->cnjk', patches, first_table))
    second_table = jnp.stack([jnp.stack([cosine, sine], 1), jnp.stack([-sine, cosine], 1)], 0).reshape(2 * length, 2, length)
    spectrum = round_half(jnp.einsum('qrn,cnjrk->cqjk', second_table, segment_one.reshape(count, length, tiles, 2, length)))
    real = spectrum[:, :length]
    imaginary = spectrum[:, length:]
    cross_real = real[:-1] * real[1:] + imaginary[:-1] * imaginary[1:]
    cross_imag = real[:-1] * imaginary[1:] - imaginary[:-1] * real[1:]
    cross = round_half(jnp.stack([cross_real, cross_imag], 1))
    third_table = jnp.stack([jnp.stack([cosine, -sine], 1), jnp.stack([sine, cosine], 1)], 0).reshape(2 * length, 2, length)
    inverse_one = round_half(jnp.einsum('qrn,crnjk->cqjk', third_table, cross))
    fourth_table = jnp.stack([cosine, -sine], 0)
    surface = jnp.einsum('crajk,rdk->cajd', inverse_one.reshape(count - 1, 2, length, tiles, length), fourth_table)
    scale = float(length) ** 3 * jnp.sqrt((energy[:-1] + 1e-05) * (energy[1:] + 1e-05))
    corr = surface / scale[:, None, :, None]
    height = lax.optimization_barrier(jnp.max(jnp.abs(corr), axis=(1, 3))) + 1e-05
    offsets = jnp.arange(WIN, dtype=jnp.int32) - WIN // 2
    positions = jnp.arange(length, dtype=jnp.int32)
    row_pick = (peak_row[:, 0, :, None] + offsets) % length
    col_pick = (peak_row[:, 1, :, None] + offsets) % length
    row_hot = (row_pick[..., None] == positions).astype(jnp.float32)
    col_hot = (col_pick[..., None] == positions).astype(jnp.float32)
    partial_rows = jnp.einsum('cjup,cpjq->cjuq', row_hot, corr, precision=lax.Precision.HIGHEST)
    window = jnp.einsum('cjuq,cjvq->cjuv', partial_rows, col_hot, precision=lax.Precision.HIGHEST)
    coefficient = jnp.einsum('euv,cjuv->cej', fit_basis(WIN), window, precision=lax.Precision.HIGHEST)
    return coefficient / height[:, None, :] * valid_row[:, None, :].astype(jnp.float32)

def reference(sections, peaks, valid):
    blank = jnp.zeros((1,) + sections.shape[1:], jnp.bfloat16)
    stacked = jnp.concatenate([sections, blank], 0)
    padded = jnp.pad(stacked, ((0, 0), (0, STRIDE), (0, STRIDE)))

    def one_row(index):
        block = lax.dynamic_slice_in_dim(padded, index * STRIDE, PATCH, axis=1)
        peak_row = lax.dynamic_index_in_dim(peaks, index, 2, False)
        valid_row = lax.dynamic_index_in_dim(valid, index, 1, False)
        return correlate_row(block, peak_row, valid_row)
    result = lax.map(one_row, jnp.arange(NPY, dtype=jnp.int32))
    return jnp.transpose(result, (1, 2, 0, 3))
```

```python
import functools
import math

import jax
import jax.numpy as jnp
import numpy as np
from jax import lax
from jax.experimental import pallas as pl
from jax.experimental.pallas import tpu as pltpu
from jax.sharding import PartitionSpec as P

PATCH = 128
STRIDE = 64
WIN = 5
HALF = PATCH // 2
F32 = jnp.float32
BF16 = jnp.bfloat16
SLOT = 16


def tables():
    index = np.arange(PATCH)
    phase = (index[:, None] * index[None, :] % PATCH).astype(np.float64) * (2.0 * math.pi / PATCH)
    cosine = np.asarray(np.cos(phase), dtype=jnp.bfloat16).astype(np.float32)
    sine = np.asarray(np.sin(phase), dtype=jnp.bfloat16).astype(np.float32)
    first = np.zeros((4 * HALF, 2 * PATCH), np.float32)
    for part, table in enumerate((cosine, -sine)):
        for which in range(2):
            top = part * PATCH + which * HALF
            first[top : top + HALF, which * STRIDE : which * STRIDE + PATCH] = table[:HALF]
    second = np.block([[cosine, -sine], [sine, cosine]])
    third = np.block([[cosine, sine], [-sine, cosine]])
    weight = np.where(np.arange(HALF) == 0, 1.0, 2.0)[None, :]
    fourth = np.concatenate(
        [cosine[:, :HALF] * weight, -sine[:, :HALF] * weight, np.repeat(cosine[:, HALF : HALF + 1], SLOT, 1)], 1
    )
    return first, second, third, fourth, cosine[HALF]


def middle_rows(middle, pairs):
    rows = np.zeros((pairs, SLOT, 2 * PATCH), np.float32)
    for pair in range(pairs):
        for which in range(2):
            rows[pair, 2 * pair + which, which * STRIDE : which * STRIDE + PATCH] = middle
    return rows


def passed_along(value, axis, steps):
    count = lax.axis_size(axis)
    initial, last = (max(0, -steps), min(count, count - steps))
    return lax.ppermute(value, axis, [(source, source + steps) for source in range(initial, last)])


def side_by_side(value):
    rows = value.shape[0] // 2
    return jnp.concatenate([value[:rows, :STRIDE], value[rows:, :STRIDE]], 1)


def lay_strip(packed_ref, into_ref, column):
    rows = packed_ref.shape[0]
    packed = packed_ref[...].astype(F32)
    low = lax.broadcasted_iota(jnp.int32, (rows, PATCH), 1) < STRIDE
    into_ref[0:rows, column : column + PATCH] = jnp.where(low, packed, 0.0).astype(BF16)
    turned = pltpu.roll(packed, STRIDE, 1)
    into_ref[rows : 2 * rows, column : column + PATCH] = jnp.where(low, turned, 0.0).astype(BF16)


def forward(image, start, first, middle, second, pair):
    lanes = slice(pair * PATCH, pair * PATCH + 2 * PATCH)
    upper = image[pl.ds(start, PATCH), lanes]
    lower = image[pl.ds(start + STRIDE, PATCH), lanes]
    left = jnp.concatenate([first[...], middle[pair]], 0)
    out = lax.dot_general(
        left, jnp.concatenate([upper, lower], 0), (((1,), (1,)), ((), ())), preferred_element_type=F32
    )
    one = out[: 2 * PATCH].astype(BF16)
    rows = [
        jnp.concatenate([one[:PATCH, w * PATCH : (w + 1) * PATCH], one[PATCH:, w * PATCH : (w + 1) * PATCH]], 1)
        for w in range(2)
    ]
    spectrum = jnp.dot(jnp.concatenate(rows, 0), second[...], preferred_element_type=F32)
    return spectrum, out[2 * PATCH :]


def forward_middle(total, second):
    value = total.astype(BF16)
    stacked = jnp.concatenate([value[:, :PATCH], value[:, PATCH:]], 0)
    return jnp.dot(stacked, second[:PATCH, :], preferred_element_type=F32)


def energies(image, sums, columns, first_row, patch_rows, out_ref, out_row):
    width = image.shape[1]

    def square(block, carry):
        pixels = image[pl.ds(pl.multiple_of(block * STRIDE, STRIDE), STRIDE), :].astype(F32)
        sums[pl.ds(block, 1), :] = jnp.sum(pixels * pixels, axis=0, keepdims=True)
        return carry

    lax.fori_loop(first_row, first_row + patch_rows + 1, square, 0)
    lane = lax.broadcasted_iota(jnp.int32, (SLOT, width), 1)
    place = lax.broadcasted_iota(jnp.int32, (SLOT, width), 0) * STRIDE
    inside = (lane >= place) & (lane < place + PATCH) & (place < columns * STRIDE)

    def gather(row, carry):
        both = sums[pl.ds(first_row + row, 1), :] + sums[pl.ds(first_row + row + 1, 1), :]
        chosen = jnp.where(inside, jnp.broadcast_to(both, (SLOT, width)), 0.0)
        value = jnp.sum(chosen, axis=1, keepdims=True) * (1.0 / (PATCH * PATCH))
        out_ref[pl.ds(pl.multiple_of((out_row + row) * SLOT, SLOT), SLOT), :] = jnp.broadcast_to(value, (SLOT, PATCH))
        return carry

    lax.fori_loop(0, patch_rows, gather, 0)


def own_kernel(
    upper_rows, active, tile, below, beside, first, middle, second, spectra, middles, energy, image, sums
):
    rows, columns = tile.shape
    patch_rows, patch_columns = rows // STRIDE, columns // STRIDE
    image[:rows, :columns] = tile[...]
    image[rows:, :columns] = below[...]
    strip = beside[...]
    low = lax.broadcasted_iota(jnp.int32, strip.shape, 1) < STRIDE
    image[:, columns:] = jnp.where(low, strip.astype(F32), 0.0).astype(BF16)
    lowest = jnp.where(active[0] > 0, 0, upper_rows // 2)
    highest = jnp.where(active[1] > 0, patch_rows // 2, upper_rows // 2)

    def two_rows(step, carry):
        start = pl.multiple_of(step * PATCH, PATCH)
        total = jnp.zeros((SLOT, 2 * PATCH), F32)
        for pair in range(patch_columns // 2):
            spectrum, part = forward(image, start, first, middle, second, pair)
            spectra[step, pair] = spectrum.astype(BF16)
            total += part
        middles[step] = forward_middle(total, second).astype(BF16)
        return carry

    lax.fori_loop(lowest, highest, two_rows, 0)
    energies(image, sums, patch_columns, 2 * lowest, 2 * (highest - lowest), energy, 2 * lowest)


def crossed(own, other, flipped):
    own = own.astype(F32)
    own_re, own_im = own[:, :PATCH], own[:, PATCH:]
    re, im = other[:, :PATCH], other[:, PATCH:]
    real = own_re * re + own_im * im
    imaginary = own_im * re - own_re * im if flipped else own_re * im - own_im * re
    return jnp.concatenate([real.astype(BF16), imaginary.astype(BF16)], 1)


def pair_kernel(
    slot, first_row, patch_rows, patch_columns, active, peaks, pieces, spectra, middles, energy,
    first, middle, second, third, fourth, out, image, sums, inverse, surface, peak, moments, offsets, other_energy
):
    flipped = slot == 1
    size = patch_rows * SLOT

    @pl.when(active[slot] == 0)
    def _():
        out[...] = jnp.zeros_like(out)

    @pl.when(active[slot] > 0)
    def _():
        bulk, edge = pieces
        rows, columns = bulk.shape
        image[:rows, :columns] = bulk[...]
        if flipped:
            blocks = columns // PATCH
            for block in range(blocks):
                image[rows:, block * PATCH : (block + 1) * PATCH] = edge[block * STRIDE : (block + 1) * STRIDE, :]
            lay_strip(edge.at[blocks * STRIDE :, :], image, columns)
        else:
            lay_strip(edge, image, columns)
        energies(image, sums, patch_columns, 0, patch_rows, other_energy, 0)
        row = lax.broadcasted_iota(jnp.int32, (SLOT, 2 * PATCH), 0)

        def two_rows(step, carry):
            start = pl.multiple_of(step * PATCH, PATCH)
            there = step + first_row // 2
            total = jnp.zeros((SLOT, 2 * PATCH), F32)
            for pair in range(patch_columns // 2):
                spectrum, part = forward(image, start, first, middle, second, pair)
                total += part
                cross = crossed(spectra[there, pair], spectrum, flipped)
                inverse[pair] = jnp.dot(cross, third[...], preferred_element_type=F32).astype(BF16)
            cross = crossed(middles[there], forward_middle(total, second), flipped)
            mid = jnp.dot(cross, third[:, :PATCH], preferred_element_type=F32)
            mid = jnp.concatenate([mid[:SLOT], mid[SLOT:]], 1)
            for column in range(patch_columns):
                top = (column % 2) * HALF
                one = inverse.at[column // 2]
                a, b = one[top : top + HALF, :], one[PATCH + top : PATCH + top + HALF, :]
                right = jnp.concatenate(
                    [
                        jnp.concatenate([a[:, :PATCH], b[:, :PATCH]], 1),
                        jnp.concatenate([a[:, PATCH:], b[:, PATCH:]], 1),
                        jnp.where(row == column, mid, 0.0).astype(BF16),
                    ],
                    0,
                )
                value = jnp.dot(fourth[...], right, preferred_element_type=F32)
                largest = jnp.max(jnp.abs(value), axis=0, keepdims=True)
                for which in range(2):
                    lanes = slice(which * PATCH, (which + 1) * PATCH)
                    surface[(2 * step + which) * patch_columns + column] = value[:, lanes]
                    peak[pl.ds((2 * step + which) * SLOT + column, 1), :] = largest[:, lanes]
            return carry

        lax.fori_loop(0, patch_rows // 2, two_rows, 0)

        def pick(i, carry):
            for column in range(patch_columns):
                at = i * SLOT + column
                down = peaks[0, i, column]
                along = peaks[1, i, column]
                offsets[pl.ds(at, 1), :] = jnp.full((1, PATCH), down, jnp.int32)
                for v in range(WIN):
                    where = (along + (v - WIN // 2 + PATCH)) & (PATCH - 1)
                    moments[v, pl.ds(at, 1), :] = surface[i * patch_columns + column, pl.ds(where, 1), :]
            return carry

        lax.fori_loop(0, patch_rows, pick, 0)
        lane = lax.broadcasted_iota(jnp.int32, (size, PATCH), 1)
        offset = (lane - offsets[:size] + (WIN // 2 + PATCH)) & (PATCH - 1)
        u = (offset - WIN // 2).astype(F32)
        within = offset < WIN
        middle_square = float(np.mean((np.arange(WIN) - WIN // 2) ** 2))
        u0 = jnp.where(within, 1.0, 0.0)
        u1 = jnp.where(within, u, 0.0)
        u2 = jnp.where(within, u * u - middle_square, 0.0)
        v0 = v1 = v2 = jnp.zeros((size, PATCH), F32)
        for v in range(WIN):
            value = moments[v, :size, :]
            position = float(v - WIN // 2)
            v0 += value
            v1 += position * value
            v2 += (position * position - middle_square) * value
        scale = float(PATCH) ** 3 * jnp.sqrt(
            (energy[first_row * SLOT : first_row * SLOT + size, 0:1] + 1e-05) * (other_energy[:size, 0:1] + 1e-05)
        )
        height = jnp.max(peak[:size], axis=1, keepdims=True) / scale + 1e-05
        numbers = np.arange(WIN) - WIN // 2
        linear = float(np.sum(numbers**2))
        quadratic = float(np.sum((numbers**2 - middle_square) ** 2))
        norms = (
            float(WIN), math.sqrt(WIN * linear), math.sqrt(WIN * linear), math.sqrt(WIN * quadratic),
            math.sqrt(WIN * quadratic), linear,
        )
        factors = ((u0, v0), (u1, v0), (u0, v1), (u2, v0), (u0, v2), (u1, v1))
        result = jnp.zeros((size, PATCH), F32)
        for e, ((fu, fv), norm) in enumerate(zip(factors, norms, strict=True)):
            coefficient = jnp.sum(fu * fv, axis=1, keepdims=True) * (1.0 / norm)
            result = jnp.where(lane == e, coefficient / scale / height, result)
        square = jnp.concatenate([result, jnp.zeros((PATCH - size, PATCH), F32)], 0) if size < PATCH else result
        out[...] = jnp.transpose(square)[:8, :]


def join_kernel(upper_rows, upper, lower, valid, out):
    count, patch_rows, patch_columns = out.shape
    for i in range(patch_rows):
        source, at = (upper, i) if i < upper_rows else (lower, i - upper_rows)
        value = source[...]
        turned = pltpu.roll(value, (PATCH - at * SLOT) % PATCH, 1) if at else value
        for e in range(count):
            out[e, i : i + 1, :] = turned[e : e + 1, :patch_columns]
    keep = valid[...].astype(F32)
    for e in range(count):
        out[e] = out[e] * keep


def body(sections, peaks, valid):
    tile = sections[0]
    rows, columns = tile.shape
    patch_rows, patch_columns = rows // STRIDE, columns // STRIDE
    pairs = patch_columns // 2
    upper_rows = (patch_rows // 2 + 1) // 2 * 2
    lower_rows = patch_rows - upper_rows
    first_lower = upper_rows * STRIDE
    upper_height = first_lower + STRIDE
    lower_height = lower_rows * STRIDE + STRIDE
    count = lax.axis_size("gz")
    position = lax.axis_index("gz")
    active = jnp.stack([position < count - 1, position > 0]).astype(jnp.int32)

    bulk_upper = passed_along(tile[:upper_height], "gz", -1)
    bulk_lower = passed_along(tile[first_lower:], "gz", 1)
    below = passed_along(tile[:STRIDE], "gy", -1)
    left = jnp.concatenate([tile[:, :PATCH], below[:, :PATCH]], 0)
    beside = passed_along(left, "gx", -1)
    edge_upper = passed_along(side_by_side(beside[:upper_height]), "gz", -1)
    edge_lower = jnp.concatenate(
        [below[:, block * PATCH : (block + 1) * PATCH] for block in range(columns // PATCH)]
        + [side_by_side(beside[first_lower:])],
        0,
    )
    edge_lower = passed_along(edge_lower, "gz", 1)
    peaks = peaks[0]
    peaks_lower = passed_along(peaks[:, upper_rows:], "gz", 1)

    first, second, third, fourth, middle = tables()
    first, second, third, fourth = (jnp.asarray(t, BF16) for t in (first, second, third, fourth))
    middle = jnp.asarray(middle_rows(middle, pairs), BF16)

    vmem = pl.BlockSpec(memory_space=pltpu.VMEM)
    smem = pl.BlockSpec(memory_space=pltpu.SMEM)
    steps = patch_rows // 2
    spectra, middles, energy = pl.pallas_call(
        functools.partial(own_kernel, upper_rows),
        out_shape=(
            jax.ShapeDtypeStruct((steps, pairs, 2 * PATCH, 2 * PATCH), BF16),
            jax.ShapeDtypeStruct((steps, 2 * SLOT, 2 * PATCH), BF16),
            jax.ShapeDtypeStruct((patch_rows * SLOT, PATCH), F32),
        ),
        in_specs=[smem] + [vmem] * 6,
        out_specs=(vmem, vmem, vmem),
        scratch_shapes=[
            pltpu.VMEM((rows + STRIDE, columns + PATCH), BF16),
            pltpu.VMEM((patch_rows + 1, columns + PATCH), F32),
        ],
        cost_estimate=pl.CostEstimate(flops=4_000_000_000, bytes_accessed=6_000_000, transcendentals=0),
        name="own",
    )(active, tile, below, beside, first, middle, second)

    def correlated(slot, first_row, count_rows, height, peaks_here, bulk, edge):
        def kernel(active, peaks, bulk, edge, *rest):
            pair_kernel(slot, first_row, count_rows, patch_columns, active, peaks, (bulk, edge), *rest)

        size = count_rows * SLOT
        return pl.pallas_call(
            kernel,
            out_shape=jax.ShapeDtypeStruct((8, PATCH), F32),
            in_specs=[smem, smem] + [vmem] * 10,
            out_specs=vmem,
            scratch_shapes=[
                pltpu.VMEM((height, columns + PATCH), BF16),
                pltpu.VMEM((count_rows + 1, columns + PATCH), F32),
                pltpu.VMEM((pairs, 2 * PATCH, 2 * PATCH), BF16),
                pltpu.VMEM((count_rows * patch_columns, PATCH, PATCH), F32),
                pltpu.VMEM((size, PATCH), F32),
                pltpu.VMEM((WIN, size, PATCH), F32),
                pltpu.VMEM((size, PATCH), jnp.int32),
                pltpu.VMEM((size, PATCH), F32),
            ],
            cost_estimate=pl.CostEstimate(flops=4_000_000_000, bytes_accessed=6_000_000, transcendentals=0),
            name=("upper", "lower")[slot],
        )(active, peaks_here, bulk, edge, spectra, middles, energy, first, middle, second, third, fourth)

    lower = correlated(1, upper_rows, lower_rows, lower_height, peaks_lower, bulk_lower, edge_lower)
    lower = passed_along(lower, "gz", -1)
    upper = correlated(0, 0, upper_rows, upper_height, peaks[:, :upper_rows], bulk_upper, edge_upper)
    fit = pl.pallas_call(
        functools.partial(join_kernel, upper_rows),
        out_shape=jax.ShapeDtypeStruct((6, patch_rows, patch_columns), F32),
        in_specs=[vmem] * 3,
        out_specs=vmem,
        name="join",
    )(upper, lower, valid[0])
    return fit[None]


def solution(mesh):
    in_specs = (P("gz", "gy", "gx"), P("gz", None, "gy", "gx"), P("gz", "gy", "gx"))
    out_specs = P("gz", None, "gy", "gx")
    return jax.shard_map(body, mesh=mesh, in_specs=in_specs, out_specs=out_specs, check_vma=False)
```

```python
import functools
import math

import jax
import jax.numpy as jnp
import numpy as np
from jax import lax
from jax.experimental import pallas as pl
from jax.experimental.pallas import tpu as pltpu
from jax.sharding import PartitionSpec as P

PATCH = 128
STRIDE = 64
WIN = 5
HALF = PATCH // 2
F32 = jnp.float32
BF16 = jnp.bfloat16
SLOT = 16


def tables():
    index = np.arange(PATCH)
    phase = (index[:, None] * index[None, :] % PATCH).astype(np.float64) * (2.0 * math.pi / PATCH)
    cosine = np.asarray(np.cos(phase), dtype=jnp.bfloat16).astype(np.float32)
    sine = np.asarray(np.sin(phase), dtype=jnp.bfloat16).astype(np.float32)
    first = np.zeros((4 * HALF, 2 * PATCH), np.float32)
    for part, table in enumerate((cosine, -sine)):
        for which in range(2):
            top = part * PATCH + which * HALF
            first[top : top + HALF, which * STRIDE : which * STRIDE + PATCH] = table[:HALF]
    second = np.block([[cosine, -sine], [sine, cosine]])
    third = np.block([[cosine, sine], [-sine, cosine]])
    weight = np.where(np.arange(HALF) == 0, 1.0, 2.0)[None, :]
    fourth = np.concatenate(
        [cosine[:, :HALF] * weight, -sine[:, :HALF] * weight, np.repeat(cosine[:, HALF : HALF + 1], SLOT, 1)], 1
    )
    return first, second, third, fourth, cosine[HALF]


def middle_rows(middle, pairs):
    rows = np.zeros((pairs, SLOT, 2 * PATCH), np.float32)
    for pair in range(pairs):
        for which in range(2):
            rows[pair, 2 * pair + which, which * STRIDE : which * STRIDE + PATCH] = middle
    return rows


def passed_along(value, axis, steps):
    count = lax.axis_size(axis)
    initial, last = (max(0, -steps), min(count, count - steps))
    return lax.ppermute(value, axis, [(source, source + steps) for source in range(initial, last)])


def side_by_side(value):
    rows = value.shape[0] // 2
    return jnp.concatenate([value[:rows, :STRIDE], value[rows:, :STRIDE]], 1)


def lay_strip(packed_ref, into_ref, column):
    rows = packed_ref.shape[0]
    packed = packed_ref[...].astype(F32)
    low = lax.broadcasted_iota(jnp.int32, (rows, PATCH), 1) < STRIDE
    into_ref[0:rows, column : column + PATCH] = jnp.where(low, packed, 0.0).astype(BF16)
    turned = pltpu.roll(packed, STRIDE, 1)
    into_ref[rows : 2 * rows, column : column + PATCH] = jnp.where(low, turned, 0.0).astype(BF16)


def forward(image, start, first, middle, second, pair):
    lanes = slice(pair * PATCH, pair * PATCH + 2 * PATCH)
    upper = image[pl.ds(start, PATCH), lanes]
    lower = image[pl.ds(start + STRIDE, PATCH), lanes]
    left = jnp.concatenate([first[...], middle[pair]], 0)
    out = lax.dot_general(
        left, jnp.concatenate([upper, lower], 0), (((1,), (1,)), ((), ())), preferred_element_type=F32
    )
    one = out[: 2 * PATCH].astype(BF16)
    rows = [
        jnp.concatenate([one[:PATCH, w * PATCH : (w + 1) * PATCH], one[PATCH:, w * PATCH : (w + 1) * PATCH]], 1)
        for w in range(2)
    ]
    spectrum = jnp.dot(jnp.concatenate(rows, 0), second[...], preferred_element_type=F32)
    return spectrum, out[2 * PATCH :]


def forward_middle(total, second):
    value = total.astype(BF16)
    stacked = jnp.concatenate([value[:, :PATCH], value[:, PATCH:]], 0)
    return jnp.dot(stacked, second[:PATCH, :], preferred_element_type=F32)


def energies(image, sums, columns, first_row, patch_rows, out_ref, out_row):
    width = image.shape[1]

    def square(block, carry):
        pixels = image[pl.ds(pl.multiple_of(block * STRIDE, STRIDE), STRIDE), :].astype(F32)
        sums[pl.ds(block, 1), :] = jnp.sum(pixels * pixels, axis=0, keepdims=True)
        return carry

    lax.fori_loop(first_row, first_row + patch_rows + 1, square, 0)
    lane = lax.broadcasted_iota(jnp.int32, (SLOT, width), 1)
    place = lax.broadcasted_iota(jnp.int32, (SLOT, width), 0) * STRIDE
    inside = (lane >= place) & (lane < place + PATCH) & (place < columns * STRIDE)

    def gather(row, carry):
        both = sums[pl.ds(first_row + row, 1), :] + sums[pl.ds(first_row + row + 1, 1), :]
        chosen = jnp.where(inside, jnp.broadcast_to(both, (SLOT, width)), 0.0)
        value = jnp.sum(chosen, axis=1, keepdims=True) * (1.0 / (PATCH * PATCH))
        out_ref[pl.ds(pl.multiple_of((out_row + row) * SLOT, SLOT), SLOT), :] = jnp.broadcast_to(value, (SLOT, PATCH))
        return carry

    lax.fori_loop(0, patch_rows, gather, 0)


def own_kernel(
    upper_rows, active, tile, below, beside, first, middle, second, spectra, middles, energy, image, sums
):
    rows, columns = tile.shape
    patch_rows, patch_columns = rows // STRIDE, columns // STRIDE
    image[:rows, :columns] = tile[...]
    image[rows:, :columns] = below[...]
    strip = beside[...]
    low = lax.broadcasted_iota(jnp.int32, strip.shape, 1) < STRIDE
    image[:, columns:] = jnp.where(low, strip.astype(F32), 0.0).astype(BF16)
    lowest = jnp.where(active[0] > 0, 0, upper_rows // 2)
    highest = jnp.where(active[1] > 0, patch_rows // 2, upper_rows // 2)

    def two_rows(step, carry):
        start = pl.multiple_of(step * PATCH, PATCH)
        total = jnp.zeros((SLOT, 2 * PATCH), F32)
        for pair in range(patch_columns // 2):
            spectrum, part = forward(image, start, first, middle, second, pair)
            spectra[step, pair] = spectrum.astype(BF16)
            total += part
        middles[step] = forward_middle(total, second).astype(BF16)
        return carry

    lax.fori_loop(lowest, highest, two_rows, 0)
    energies(image, sums, patch_columns, 2 * lowest, 2 * (highest - lowest), energy, 2 * lowest)


def crossed(own, other, flipped):
    own = own.astype(F32)
    own_re, own_im = own[:, :PATCH], own[:, PATCH:]
    re, im = other[:, :PATCH], other[:, PATCH:]
    real = own_re * re + own_im * im
    imaginary = own_im * re - own_re * im if flipped else own_re * im - own_im * re
    return jnp.concatenate([real.astype(BF16), imaginary.astype(BF16)], 1)


def pair_kernel(
    slot, first_row, patch_rows, patch_columns, active, peaks, pieces, spectra, middles, energy,
    first, middle, second, third, fourth, out, image, sums, inverse, surface, peak, moments, offsets, other_energy
):
    flipped = slot == 1
    size = patch_rows * SLOT

    @pl.when(active[slot] == 0)
    def _():
        out[...] = jnp.zeros_like(out)

    @pl.when(active[slot] > 0)
    def _():
        bulk, edge = pieces
        rows, columns = bulk.shape
        image[:rows, :columns] = bulk[...]
        if flipped:
            blocks = columns // PATCH
            for block in range(blocks):
                image[rows:, block * PATCH : (block + 1) * PATCH] = edge[block * STRIDE : (block + 1) * STRIDE, :]
            lay_strip(edge.at[blocks * STRIDE :, :], image, columns)
        else:
            lay_strip(edge, image, columns)
        energies(image, sums, patch_columns, 0, patch_rows, other_energy, 0)
        row = lax.broadcasted_iota(jnp.int32, (SLOT, 2 * PATCH), 0)

        def two_rows(step, carry):
            start = pl.multiple_of(step * PATCH, PATCH)
            there = step + first_row // 2
            total = jnp.zeros((SLOT, 2 * PATCH), F32)
            for pair in range(patch_columns // 2):
                spectrum, part = forward(image, start, first, middle, second, pair)
                total += part
                cross = crossed(spectra[there, pair], spectrum, flipped)
                inverse[pair] = jnp.dot(cross, third[...], preferred_element_type=F32).astype(BF16)
            cross = crossed(middles[there], forward_middle(total, second), flipped)
            mid = jnp.dot(cross, third[:, :PATCH], preferred_element_type=F32)
            mid = jnp.concatenate([mid[:SLOT], mid[SLOT:]], 1)
            for column in range(patch_columns):
                top = (column % 2) * HALF
                one = inverse.at[column // 2]
                a, b = one[top : top + HALF, :], one[PATCH + top : PATCH + top + HALF, :]
                right = jnp.concatenate(
                    [
                        jnp.concatenate([a[:, :PATCH], b[:, :PATCH]], 1),
                        jnp.concatenate([a[:, PATCH:], b[:, PATCH:]], 1),
                        jnp.where(row == column, mid, 0.0).astype(BF16),
                    ],
                    0,
                )
                value = jnp.dot(fourth[...], right, preferred_element_type=F32)
                largest = jnp.max(jnp.abs(value), axis=0, keepdims=True)
                for which in range(2):
                    lanes = slice(which * PATCH, (which + 1) * PATCH)
                    surface[(2 * step + which) * patch_columns + column] = value[:, lanes]
                    peak[pl.ds((2 * step + which) * SLOT + column, 1), :] = largest[:, lanes]
            return carry

        lax.fori_loop(0, patch_rows // 2, two_rows, 0)

        def pick(i, carry):
            for column in range(patch_columns):
                at = i * SLOT + column
                down = peaks[0, i, column]
                along = peaks[1, i, column]
                offsets[pl.ds(at, 1), :] = jnp.full((1, PATCH), down, jnp.int32)
                for v in range(WIN):
                    where = (along + (v - WIN // 2 + PATCH)) & (PATCH - 1)
                    moments[v, pl.ds(at, 1), :] = surface[i * patch_columns + column, pl.ds(where, 1), :]
            return carry

        lax.fori_loop(0, patch_rows, pick, 0)
        lane = lax.broadcasted_iota(jnp.int32, (size, PATCH), 1)
        offset = (lane - offsets[:size] + (WIN // 2 + PATCH)) & (PATCH - 1)
        u = (offset - WIN // 2).astype(F32)
        within = offset < WIN
        middle_square = float(np.mean((np.arange(WIN) - WIN // 2) ** 2))
        u0 = jnp.where(within, 1.0, 0.0)
        u1 = jnp.where(within, u, 0.0)
        u2 = jnp.where(within, u * u - middle_square, 0.0)
        v0 = v1 = v2 = jnp.zeros((size, PATCH), F32)
        for v in range(WIN):
            value = moments[v, :size, :]
            position = float(v - WIN // 2)
            v0 += value
            v1 += position * value
            v2 += (position * position - middle_square) * value
        scale = float(PATCH) ** 3 * jnp.sqrt(
            (energy[first_row * SLOT : first_row * SLOT + size, 0:1] + 1e-05) * (other_energy[:size, 0:1] + 1e-05)
        )
        height = jnp.max(peak[:size], axis=1, keepdims=True) / scale + 1e-05
        numbers = np.arange(WIN) - WIN // 2
        linear = float(np.sum(numbers**2))
        quadratic = float(np.sum((numbers**2 - middle_square) ** 2))
        norms = (
            float(WIN), math.sqrt(WIN * linear), math.sqrt(WIN * linear), math.sqrt(WIN * quadratic),
            math.sqrt(WIN * quadratic), linear,
        )
        factors = ((u0, v0), (u1, v0), (u0, v1), (u2, v0), (u0, v2), (u1, v1))
        result = jnp.zeros((size, PATCH), F32)
        for e, ((fu, fv), norm) in enumerate(zip(factors, norms, strict=True)):
            coefficient = jnp.sum(fu * fv, axis=1, keepdims=True) * (1.0 / norm)
            result = jnp.where(lane == e, coefficient / scale / height, result)
        square = jnp.concatenate([result, jnp.zeros((PATCH - size, PATCH), F32)], 0) if size < PATCH else result
        out[...] = jnp.transpose(square)[:8, :]


def join_kernel(upper_rows, upper, lower, valid, out):
    count, patch_rows, patch_columns = out.shape
    for i in range(patch_rows):
        source, at = (upper, i) if i < upper_rows else (lower, i - upper_rows)
        value = source[...]
        turned = pltpu.roll(value, (PATCH - at * SLOT) % PATCH, 1) if at else value
        for e in range(count):
            out[e, i : i + 1, :] = turned[e : e + 1, :patch_columns]
    keep = valid[...].astype(F32)
    for e in range(count):
        out[e] = out[e] * keep


def body(sections, peaks, valid):
    tile = sections[0]
    rows, columns = tile.shape
    patch_rows, patch_columns = rows // STRIDE, columns // STRIDE
    pairs = patch_columns // 2
    upper_rows = (patch_rows // 2 + 1) // 2 * 2
    lower_rows = patch_rows - upper_rows
    first_lower = upper_rows * STRIDE
    upper_height = first_lower + STRIDE
    lower_height = lower_rows * STRIDE + STRIDE
    count = lax.axis_size("gz")
    position = lax.axis_index("gz")
    active = jnp.stack([position < count - 1, position > 0]).astype(jnp.int32)

    bulk_upper = passed_along(tile[:upper_height], "gz", -1)
    bulk_lower = passed_along(tile[first_lower:], "gz", 1)
    below = passed_along(tile[:STRIDE], "gy", -1)
    left = jnp.concatenate([tile[:, :PATCH], below[:, :PATCH]], 0)
    beside = passed_along(left, "gx", -1)
    edge_upper = passed_along(side_by_side(beside[:upper_height]), "gz", -1)
    edge_lower = jnp.concatenate(
        [below[:, block * PATCH : (block + 1) * PATCH] for block in range(columns // PATCH)]
        + [side_by_side(beside[first_lower:])],
        0,
    )
    edge_lower = passed_along(edge_lower, "gz", 1)
    peaks = peaks[0]
    peaks_lower = passed_along(peaks[:, upper_rows:], "gz", 1)

    first, second, third, fourth, middle = tables()
    first, second, third, fourth = (jnp.asarray(t, BF16) for t in (first, second, third, fourth))
    middle = jnp.asarray(middle_rows(middle, pairs), BF16)

    vmem = pl.BlockSpec(memory_space=pltpu.VMEM)
    smem = pl.BlockSpec(memory_space=pltpu.SMEM)
    steps = patch_rows // 2
    spectra, middles, energy = pl.pallas_call(
        functools.partial(own_kernel, upper_rows),
        out_shape=(
            jax.ShapeDtypeStruct((steps, pairs, 2 * PATCH, 2 * PATCH), BF16),
            jax.ShapeDtypeStruct((steps, 2 * SLOT, 2 * PATCH), BF16),
            jax.ShapeDtypeStruct((patch_rows * SLOT, PATCH), F32),
        ),
        in_specs=[smem] + [vmem] * 6,
        out_specs=(vmem, vmem, vmem),
        scratch_shapes=[
            pltpu.VMEM((rows + STRIDE, columns + PATCH), BF16),
            pltpu.VMEM((patch_rows + 1, columns + PATCH), F32),
        ],
        cost_estimate=pl.CostEstimate(flops=4_000_000_000, bytes_accessed=6_000_000, transcendentals=0),
        name="own", compiler_params=pltpu.CompilerParams(vmem_limit_bytes=8 << 20),
    )(active, tile, below, beside, first, middle, second)

    def correlated(slot, first_row, count_rows, height, peaks_here, bulk, edge):
        def kernel(active, peaks, bulk, edge, *rest):
            pair_kernel(slot, first_row, count_rows, patch_columns, active, peaks, (bulk, edge), *rest)

        size = count_rows * SLOT
        return pl.pallas_call(
            kernel,
            out_shape=jax.ShapeDtypeStruct((8, PATCH), F32),
            in_specs=[smem, smem] + [vmem] * 10,
            out_specs=vmem,
            scratch_shapes=[
                pltpu.VMEM((height, columns + PATCH), BF16),
                pltpu.VMEM((count_rows + 1, columns + PATCH), F32),
                pltpu.VMEM((pairs, 2 * PATCH, 2 * PATCH), BF16),
                pltpu.VMEM((count_rows * patch_columns, PATCH, PATCH), F32),
                pltpu.VMEM((size, PATCH), F32),
                pltpu.VMEM((WIN, size, PATCH), F32),
                pltpu.VMEM((size, PATCH), jnp.int32),
                pltpu.VMEM((size, PATCH), F32),
            ],
            cost_estimate=pl.CostEstimate(flops=4_000_000_000, bytes_accessed=6_000_000, transcendentals=0),
            name=("upper", "lower")[slot], compiler_params=pltpu.CompilerParams(vmem_limit_bytes=12 << 20),
        )(active, peaks_here, bulk, edge, spectra, middles, energy, first, middle, second, third, fourth)

    lower = correlated(1, upper_rows, lower_rows, lower_height, peaks_lower, bulk_lower, edge_lower)
    lower = passed_along(lower, "gz", -1)
    upper = correlated(0, 0, upper_rows, upper_height, peaks[:, :upper_rows], bulk_upper, edge_upper)
    fit = pl.pallas_call(
        functools.partial(join_kernel, upper_rows),
        out_shape=jax.ShapeDtypeStruct((6, patch_rows, patch_columns), F32),
        in_specs=[vmem] * 3,
        out_specs=vmem,
        name="join", compiler_params=pltpu.CompilerParams(vmem_limit_bytes=1 << 20),
    )(upper, lower, valid[0])
    return fit[None]


def solution(mesh):
    in_specs = (P("gz", "gy", "gx"), P("gz", None, "gy", "gx"), P("gz", "gy", "gx"))
    out_specs = P("gz", None, "gy", "gx")
    return jax.shard_map(body, mesh=mesh, in_specs=in_specs, out_specs=out_specs, check_vma=False)
```

```python
import functools
import math

import jax
import jax.numpy as jnp
import numpy as np
from jax import lax
from jax.experimental import pallas as pl
from jax.experimental.pallas import tpu as pltpu
from jax.sharding import PartitionSpec as P

PATCH = 128
STRIDE = 64
WIN = 5
HALF = PATCH // 2
EDGE = 8
SLOT = 16
PARTS = 2
F32 = jnp.float32
BF16 = jnp.bfloat16


def tables():
    index = np.arange(PATCH)
    phase = (index[:, None] * index[None, :] % PATCH).astype(np.float64) * (2.0 * math.pi / PATCH)
    cosine = np.asarray(np.cos(phase), dtype=jnp.bfloat16).astype(np.float32)
    sine = np.asarray(np.sin(phase), dtype=jnp.bfloat16).astype(np.float32)
    first = np.zeros((4 * HALF, 2 * PATCH), np.float32)
    for part, table in enumerate((cosine, -sine)):
        for which in range(2):
            top = part * PATCH + which * HALF
            first[top : top + HALF, which * STRIDE : which * STRIDE + PATCH] = table[:HALF]
    second = np.block([[cosine, -sine], [sine, cosine]])
    third = np.block([[cosine, sine], [-sine, cosine]])
    weight = np.where(np.arange(HALF) == 0, 1.0, 2.0)[None, :]
    fourth = np.concatenate(
        [cosine[:, :HALF] * weight, -sine[:, :HALF] * weight, np.repeat(cosine[:, HALF : HALF + 1], SLOT, 1)], 1
    )
    return first, second, third, fourth, cosine[HALF]


def middle_rows(middle, pairs):
    rows = np.zeros((pairs, SLOT, 2 * PATCH), np.float32)
    for pair in range(pairs):
        for which in range(2):
            rows[pair, 2 * pair + which, which * STRIDE : which * STRIDE + PATCH] = middle
    return rows


def columns_mask(blocks, columns):
    mask = np.zeros((blocks * PATCH, PATCH), np.float32)
    for column in range(columns):
        mask[column * STRIDE : column * STRIDE + PATCH, column] = 1.0
    return mask


def passed_along(value, axis, steps):
    count = lax.axis_size(axis)
    initial, last = (max(0, -steps), min(count, count - steps))
    return lax.ppermute(value, axis, [(source, source + steps) for source in range(initial, last)])


def side_by_side(value):
    rows = value.shape[0] // 2
    return jnp.concatenate([value[:rows, :STRIDE], value[rows:, :STRIDE]], 1)


def two_terms(value):
    high = value.astype(BF16)
    return high, (value - high.astype(F32)).astype(BF16)


def only_low(value):
    low = lax.broadcasted_iota(jnp.int32, value.shape, 1) < STRIDE
    return jnp.where(low, value.astype(F32), 0.0).astype(BF16)


def parts(rows):
    step = rows // PARTS
    return [slice(top, top + step) for top in range(0, rows, step)]


def window_of(chunk, start, block):
    return jnp.concatenate([chunk(start, block), chunk(start + 1, block)], 0)


def forward(chunk, start, first, middle, columns_of):
    pairs = middle.shape[0]
    total = jnp.zeros((SLOT, 2 * PATCH), F32)
    for pair in range(pairs):
        right = jnp.concatenate(
            [
                jnp.concatenate([window_of(chunk, start + w, pair + half) for half in range(2)], 1)
                for w in range(2)
            ],
            0,
        )
        left = jnp.concatenate([first[...], middle[pair]], 0)
        out = lax.dot_general(left, right, (((1,), (1,)), ((), ())), preferred_element_type=F32)
        one = out[: 2 * PATCH].astype(BF16)
        for w in range(2):
            top = (2 * pair + w) * PATCH
            columns_of[top : top + PATCH, :PATCH] = one[:PATCH, w * PATCH : (w + 1) * PATCH]
            columns_of[top : top + PATCH, PATCH:] = one[PATCH:, w * PATCH : (w + 1) * PATCH]
        total += out[2 * PATCH :]
    value = total.astype(BF16)
    top = 2 * pairs * PATCH
    for w in range(2):
        columns_of[top + w * SLOT : top + (w + 1) * SLOT, :PATCH] = value[:, w * PATCH : (w + 1) * PATCH]
    columns_of[top : top + 2 * SLOT, PATCH:] = jnp.zeros((2 * SLOT, PATCH), BF16)


def energies(chunk, blocks, first_row, patch_rows, mask, sums):
    for row in range(patch_rows + 1):
        for block in range(blocks):
            pixels = chunk(first_row + row, block).astype(F32)
            sums[row : row + 1, block * PATCH : (block + 1) * PATCH] = jnp.sum(pixels * pixels, axis=0, keepdims=True)
    both = sums[0:patch_rows, :] + sums[1 : patch_rows + 1, :]
    total = sum(jnp.dot(term, mask[...], preferred_element_type=F32) for term in two_terms(both))
    return total * (1.0 / (PATCH * PATCH))


def prepare_kernel(upper_rows, merged, active, tile, peaks, *outs):
    rows, columns = tile.shape
    patch_rows = rows // STRIDE
    height = (upper_rows + 1) * STRIDE
    first_lower = upper_rows * STRIDE
    lower = rows - first_lower
    top, left, packed = outs[-3:]

    def upwards(early, late):
        early[...] = tile[:height, :PATCH]
        late[...] = tile[:height, PATCH:]

    def downwards(early, late):
        blocks = columns // PATCH
        for block in range(blocks):
            early[block * STRIDE : (block + 1) * STRIDE, :] = tile[:STRIDE, block * PATCH : (block + 1) * PATCH]
        wide = late.shape[1]
        late[:lower, :] = tile[first_lower:, :wide]
        for half in range(2):
            late[lower : lower + lower // 2, half * PATCH : (half + 1) * PATCH] = tile[
                first_lower + half * lower // 2 : first_lower + (half + 1) * lower // 2, wide:
            ]
        packed[...] = jnp.zeros_like(packed)
        for i in range(patch_rows - upper_rows):
            packed[2 * i : 2 * i + 2, : peaks.shape[2]] = peaks[upper_rows + i].astype(F32)
        late[lower + lower // 2 : lower + lower // 2 + SLOT, :PATCH] = packed[...].astype(BF16)

    if merged:
        pl.when(active[1] > 0)(lambda: upwards(*outs[:2]))
        pl.when(active[1] == 0)(lambda: downwards(*outs[:2]))
    else:
        upwards(*outs[:2])
        downwards(*outs[2:4])
    top[...] = tile[:STRIDE, :]
    left[...] = tile[:, :PATCH]


def own_kernel(
    upper_rows, active, tile, below, beside, first, middle, second, mask, spectra, energy, strip, sums, once
):
    rows, columns = tile.shape
    patch_rows = rows // STRIDE
    blocks = columns // PATCH
    strip[...] = only_low(beside[: rows + STRIDE, :])

    def chunk(row, block):
        at = slice(row * STRIDE, (row + 1) * STRIDE)
        if block == blocks:
            return strip[at, :]
        lanes = slice(block * PATCH, (block + 1) * PATCH)
        return tile[at, lanes] if row < patch_rows else below[:, lanes]

    for slot, (lowest, highest) in enumerate(((0, upper_rows), (upper_rows, patch_rows))):

        @pl.when(active[slot] > 0)
        def _(slot=slot, lowest=lowest, highest=highest):
            for step in range(lowest // 2, highest // 2):
                columns_of = once.at[step % 2]
                forward(chunk, 2 * step, first, middle, columns_of)
                for part in parts(columns_of.shape[0]):
                    value = jnp.dot(columns_of[part, :], second[...], preferred_element_type=F32)
                    spectra[step, part, :] = value.astype(BF16)
            energy[slot, : highest - lowest, :] = energies(
                chunk, blocks + 1, lowest, highest - lowest, mask, sums
            )


def crossed(own, other, flipped):
    own = own.astype(F32)
    own_re, own_im = own[:, :PATCH], own[:, PATCH:]
    re, im = other[:, :PATCH], other[:, PATCH:]
    real = own_re * re + own_im * im
    imaginary = own_im * re - own_re * im if flipped else own_re * im - own_im * re
    return jnp.concatenate([real.astype(BF16), imaginary.astype(BF16)], 1)


def pair_kernel(
    slot, first_row, patch_rows, patch_columns, active, peaks, early, late, beside, spectra, energy,
    first, middle, second, third, fourth, mask, out, strip, sums, once, crosses, inverse, peak, moments, offsets,
    *surfaces
):
    flipped = slot == 1
    size = patch_rows * SLOT
    pairs = patch_columns // 2
    blocks = pairs

    @pl.when(active[slot] == 0)
    def _():
        out[...] = jnp.zeros_like(out)

    @pl.when(active[slot] > 0)
    def _():
        if flipped:
            half = strip.shape[0] // 2
            packed = beside[...].astype(F32)
            low = lax.broadcasted_iota(jnp.int32, packed.shape, 1) < STRIDE
            strip[:half, :] = jnp.where(low, packed, 0.0).astype(BF16)
            strip[half:, :] = jnp.where(low, pltpu.roll(packed, STRIDE, 1), 0.0).astype(BF16)
        else:
            strip[...] = only_low(beside[beside.shape[0] - strip.shape[0] :, :])

        def chunk(row, block):
            at = slice(row * STRIDE, (row + 1) * STRIDE)
            if block == blocks:
                return strip[at, :]
            if not flipped:
                return early[at, :] if block == 0 else late[at, (block - 1) * PATCH : block * PATCH]
            if row == patch_rows:
                return early[block * STRIDE : (block + 1) * STRIDE, :]
            if block < blocks - 1:
                return late[at, block * PATCH : (block + 1) * PATCH]
            side, place = divmod(row, patch_rows // 2)
            top = (patch_rows + place) * STRIDE
            return late[top : top + STRIDE, side * PATCH : (side + 1) * PATCH]

        row_of = lax.broadcasted_iota(jnp.int32, (SLOT, 2 * PATCH), 0)
        for step in range(patch_rows // 2):
            columns_of, cross, back = once.at[step % 2], crosses.at[step % 2], inverse.at[step % 2]
            forward(chunk, 2 * step, first, middle, columns_of)
            for part in parts(columns_of.shape[0]):
                spectrum = jnp.dot(columns_of[part, :], second[...], preferred_element_type=F32)
                cross[part, :] = crossed(spectra[step + first_row // 2, part, :], spectrum, flipped)
            for part in parts(columns_of.shape[0]):
                back[part, :] = jnp.dot(cross[part, :], third[...], preferred_element_type=F32).astype(BF16)
            top = 2 * pairs * PATCH
            mid = back[top : top + 2 * SLOT, :PATCH].astype(F32)
            mid = jnp.concatenate([mid[:SLOT], mid[SLOT:]], 1)
            for column in range(patch_columns):
                a = (column // 2) * 2 * PATCH + (column % 2) * HALF
                b = a + PATCH
                right = jnp.concatenate(
                    [
                        jnp.concatenate([back[a : a + HALF, :PATCH], back[b : b + HALF, :PATCH]], 1),
                        jnp.concatenate([back[a : a + HALF, PATCH:], back[b : b + HALF, PATCH:]], 1),
                        jnp.where(row_of == column, mid, 0.0).astype(BF16),
                    ],
                    0,
                )
                value = jnp.dot(fourth[...], right, preferred_element_type=F32)
                largest = jnp.max(jnp.abs(value), axis=0, keepdims=True)
                for which in range(2):
                    lanes = slice(which * PATCH, (which + 1) * PATCH)
                    i = 2 * step + which
                    at = i * SLOT + column
                    surface = surfaces[2 * column + which]
                    surface[EDGE : EDGE + PATCH, :] = value[:, lanes]
                    surface[:EDGE, :] = value[PATCH - EDGE :, lanes]
                    surface[EDGE + PATCH :, :] = value[:EDGE, lanes]
                    peak[at : at + 1, :] = largest[:, lanes]
                    along = peaks[i, 1, column] + (EDGE - WIN // 2)
                    moments[at * 8 : at * 8 + 8, :] = surface[pl.ds(along, 8), :]
                    offsets[at : at + 1, :] = jnp.full((1, PATCH), peaks[i, 0, column], jnp.int32)
        other = energies(chunk, blocks + 1, 0, patch_rows, mask, sums)
        scales = float(PATCH) ** 3 * jnp.sqrt((energy[slot, :patch_rows, :] + 1e-05) * (other + 1e-05))

        lane = lax.broadcasted_iota(jnp.int32, (1, PATCH), 1)
        scale = jnp.ones((1, PATCH), F32)
        for i in range(patch_rows):
            row = scales[i : i + 1, :]
            row = pltpu.roll(row, i * SLOT, 1) if i else row
            scale = jnp.where((lane >= i * SLOT) & (lane < i * SLOT + patch_columns), row, scale)
        peak_rows = peak[...]
        height = jnp.max(jnp.transpose(peak_rows), axis=0, keepdims=True) / scale + 1e-05

        lane = lax.broadcasted_iota(jnp.int32, (size, PATCH), 1)
        offset = (lane - offsets[...] + (WIN // 2 + PATCH)) & (PATCH - 1)
        u = (offset - WIN // 2).astype(F32)
        within = offset < WIN
        numbers = np.arange(WIN) - WIN // 2
        middle_square = float(np.mean(numbers**2))
        u0 = jnp.where(within, 1.0, 0.0)
        u1 = jnp.where(within, u, 0.0)
        u2 = jnp.where(within, u * u - middle_square, 0.0)
        v0 = v1 = v2 = jnp.zeros((size, PATCH), F32)
        for v in range(WIN):
            value = moments[pl.ds(v, size, stride=8), :]
            position = float(v - WIN // 2)
            v0 += value
            v1 += position * value
            v2 += (position * position - middle_square) * value
        factors = ((u0, v0), (u1, v0), (u0, v1), (u2, v0), (u0, v2), (u1, v1))
        terms = [two_terms(fu * fv) for fu, fv in factors]
        which_e = lax.broadcasted_iota(jnp.int32, (SLOT, len(terms) * PATCH), 0)
        of_lane = lax.broadcasted_iota(jnp.int32, (SLOT, len(terms) * PATCH), 1)
        ones = jnp.where((of_lane >= which_e * PATCH) & (of_lane < (which_e + 1) * PATCH), 1.0, 0.0).astype(BF16)
        total = sum(
            lax.dot_general(
                ones, jnp.concatenate([t[k] for t in terms], 1), (((1,), (1,)), ((), ())), preferred_element_type=F32
            )
            for k in range(2)
        )[:8]
        linear = float(np.sum(numbers**2))
        quadratic = float(np.sum((numbers**2 - middle_square) ** 2))
        norms = (
            float(WIN), math.sqrt(WIN * linear), math.sqrt(WIN * linear), math.sqrt(WIN * quadratic),
            math.sqrt(WIN * quadratic), linear,
        )
        e_row = lax.broadcasted_iota(jnp.int32, (8, size), 0)
        factor = jnp.zeros((8, size), F32)
        for e, norm in enumerate(norms):
            factor = jnp.where(e_row == e, 1.0 / norm, factor)
        out[:, :size] = total * factor / (scale * height)[:, :size]
        if size < PATCH:
            out[:, size:] = jnp.zeros((8, PATCH - size), F32)


def join_kernel(upper_rows, upper, lower, valid, out):
    count, patch_rows, _, patch_columns = out.shape
    for i in range(patch_rows):
        source, at = (upper, i) if i < upper_rows else (lower, i - upper_rows)
        value = source[...]
        turned = pltpu.roll(value, PATCH - at * SLOT, 1) if at else value
        keep = valid[i].astype(F32)
        for e in range(count):
            out[e, i] = turned[e : e + 1, :patch_columns] * keep


def body(sections, peaks, valid):
    tile = sections[0]
    rows, columns = tile.shape
    patch_rows, patch_columns = rows // STRIDE, columns // STRIDE
    pairs = patch_columns // 2
    upper_rows = (patch_rows // 2 + 1) // 2 * 2
    lower_rows = patch_rows - upper_rows
    first_lower = upper_rows * STRIDE
    upper_height = first_lower + STRIDE
    lower_height = lower_rows * STRIDE + STRIDE
    count, height = lax.axis_size("gz"), lax.axis_size("gy")
    position = lax.axis_index("gz")
    active = jnp.stack([position < count - 1, position > 0]).astype(jnp.int32)
    peaks = jnp.transpose(peaks, (0, 2, 1, 3))[0]
    valid = jnp.transpose(valid, (1, 0, 2))

    first, second, third, fourth, middle = tables()
    first, second, third, fourth = (jnp.asarray(t, BF16) for t in (first, second, third, fourth))
    middle = jnp.asarray(middle_rows(middle, pairs), BF16)
    mask = jnp.asarray(columns_mask(columns // PATCH + 1, patch_columns), BF16)

    vmem = pl.BlockSpec(memory_space=pltpu.VMEM)
    smem = pl.BlockSpec(memory_space=pltpu.SMEM)

    def grant(mib):
        return pltpu.CompilerParams(vmem_limit_bytes=mib << 20)

    def shape(*dims, dtype=BF16):
        return jax.ShapeDtypeStruct(dims, dtype)

    merged = count == 2
    early, late = shape(upper_height, PATCH), shape(upper_height, columns - PATCH)
    outs = pl.pallas_call(
        functools.partial(prepare_kernel, upper_rows, merged),
        out_shape=((early, late) if merged else (early, late) * 2) + (shape(STRIDE, columns), shape(rows, PATCH)),
        in_specs=[smem, vmem, vmem],
        out_specs=(vmem,) * (4 if merged else 6),
        scratch_shapes=[pltpu.VMEM((SLOT, PATCH), F32)],
        compiler_params=grant(2),
        name="prepare",
    )(active, tile, peaks)
    top, left = outs[-2:]

    up = [((s + 1) * height + y, s * height + y) for s in range(count - 1) for y in range(height)]
    down = [(s * height + y + 1, (s + 1) * height + y) for s in range(count - 1) for y in range(height - 1)]
    if merged:
        early_upper = early_lower = lax.ppermute(outs[0], ("gz", "gy"), up + down)
        late_upper = late_lower = lax.ppermute(outs[1], "gz", [(0, 1), (1, 0)])
    else:
        early_upper = lax.ppermute(outs[0], ("gz", "gy"), up)
        early_lower = lax.ppermute(outs[2], ("gz", "gy"), down)
        late_upper = passed_along(outs[1], "gz", -1)
        late_lower = passed_along(outs[3], "gz", 1)
    below = passed_along(top, "gy", -1)
    beside = passed_along(jnp.concatenate([left, below[:, :PATCH], early_upper], 0), "gx", -1)
    edge_lower = passed_along(side_by_side(beside[first_lower : rows + STRIDE]), "gz", 1)

    steps = patch_rows // 2
    depth = 2 * pairs * PATCH + 2 * SLOT
    width = columns + PATCH
    spectra, energy = pl.pallas_call(
        functools.partial(own_kernel, upper_rows),
        out_shape=(shape(steps, depth, 2 * PATCH), shape(2, 8, PATCH, dtype=F32)),
        in_specs=[smem] + [vmem] * 7,
        out_specs=(vmem, vmem),
        scratch_shapes=[
            pltpu.VMEM((rows + STRIDE, PATCH), BF16),
            pltpu.VMEM((8, width), F32),
            pltpu.VMEM((2, depth, 2 * PATCH), BF16),
        ],
        compiler_params=grant(6),
        cost_estimate=pl.CostEstimate(flops=2_000_000_000, bytes_accessed=6_000_000, transcendentals=0),
        name="own",
    )(active, tile, below, beside, first, middle, second, mask)

    def correlated(slot, first_row, count_rows, strip_rows, peaks_here, early, late, beside):
        size = count_rows * SLOT
        return pl.pallas_call(
            functools.partial(pair_kernel, slot, first_row, count_rows, patch_columns),
            out_shape=shape(8, PATCH, dtype=F32),
            in_specs=[smem, smem] + [vmem] * 11,
            out_specs=vmem,
            scratch_shapes=[
                pltpu.VMEM((strip_rows, PATCH), BF16),
                pltpu.VMEM((8, width), F32),
                pltpu.VMEM((2, depth, 2 * PATCH), BF16),
                pltpu.VMEM((2, depth, 2 * PATCH), BF16),
                pltpu.VMEM((2, depth, 2 * PATCH), BF16),
                pltpu.VMEM((PATCH, PATCH), F32),
                pltpu.VMEM((size * 8, PATCH), F32),
                pltpu.VMEM((size, PATCH), jnp.int32),
            ]
            + [pltpu.VMEM((PATCH + 2 * EDGE, PATCH), F32)] * (2 * patch_columns),
            compiler_params=grant(12),
            cost_estimate=pl.CostEstimate(flops=4_000_000_000, bytes_accessed=6_000_000, transcendentals=0),
            name=("upper", "lower")[slot],
        )(active, peaks_here, early, late, beside, spectra, energy, first, middle, second, third, fourth, mask)

    at = lower_rows * STRIDE + lower_rows * STRIDE // 2
    peaks_lower = late_lower[at : at + 2 * lower_rows, :patch_columns].astype(jnp.int32)
    peaks_lower = peaks_lower.reshape(lower_rows, 2, patch_columns)
    lower = correlated(1, upper_rows, lower_rows, lower_height, peaks_lower, early_lower, late_lower, edge_lower)
    lower = passed_along(lower, "gz", -1)
    upper = correlated(0, 0, upper_rows, upper_height, peaks, early_upper, late_upper, beside)
    fit = pl.pallas_call(
        functools.partial(join_kernel, upper_rows),
        out_shape=shape(6, patch_rows, 1, patch_columns, dtype=F32),
        in_specs=[vmem] * 3,
        out_specs=vmem,
        compiler_params=grant(1),
        name="join",
    )(upper, lower, valid)
    return jnp.transpose(fit, (2, 0, 1, 3))


def solution(mesh):
    in_specs = (P("gz", "gy", "gx"), P("gz", None, "gy", "gx"), P("gz", "gy", "gx"))
    out_specs = P("gz", None, "gy", "gx")
    return jax.shard_map(body, mesh=mesh, in_specs=in_specs, out_specs=out_specs, check_vma=False)
```

```python
import functools
import math

import jax
import jax.numpy as jnp
import numpy as np
from jax import lax
from jax.experimental import pallas as pl
from jax.experimental.pallas import tpu as pltpu
from jax.sharding import PartitionSpec as P


PATCH = 128
STRIDE = 64
WIN = 5
HALF = PATCH // 2
EDGE = 8
SLOT = 16
PARTS = 2
F32 = jnp.float32
BF16 = jnp.bfloat16


def tables():
    index = np.arange(PATCH)
    phase = (index[:, None] * index[None, :] % PATCH).astype(np.float64) * (2.0 * math.pi / PATCH)
    cosine = np.asarray(np.cos(phase), dtype=jnp.bfloat16).astype(np.float32)
    sine = np.asarray(np.sin(phase), dtype=jnp.bfloat16).astype(np.float32)
    first = np.zeros((4 * HALF, 2 * PATCH), np.float32)
    for part, table in enumerate((cosine, -sine)):
        for which in range(2):
            top = part * PATCH + which * HALF
            first[top : top + HALF, which * STRIDE : which * STRIDE + PATCH] = table[:HALF]
    second = np.block([[cosine, -sine], [sine, cosine]])
    third = np.block([[cosine, sine], [-sine, cosine]])
    weight = np.where(np.arange(HALF) == 0, 1.0, 2.0)[None, :]
    fourth = np.concatenate(
        [cosine[:, :HALF] * weight, -sine[:, :HALF] * weight, np.repeat(cosine[:, HALF : HALF + 1], SLOT, 1)], 1
    )
    return first, second, third, fourth, cosine[HALF]


def middle_rows(middle, pairs):
    rows = np.zeros((pairs, SLOT, 2 * PATCH), np.float32)
    for pair in range(pairs):
        for which in range(2):
            rows[pair, 2 * pair + which, which * STRIDE : which * STRIDE + PATCH] = middle
    return rows


def columns_mask(blocks, columns):
    mask = np.zeros((blocks * PATCH, PATCH), np.float32)
    for column in range(columns):
        mask[column * STRIDE : column * STRIDE + PATCH, column] = 1.0
    return mask


class Tables:
    def __init__(self, ref, pairs):
        self.ref, self.pairs = ref, pairs

    def rows(self, top, count):
        return self.ref[top : top + count, :]

    def first(self):
        return self.rows(0, 2 * PATCH)

    def middle(self, pair):
        return self.rows(6 * PATCH + PATCH + pair * SLOT, SLOT)

    def second(self):
        return self.rows(2 * PATCH, 2 * PATCH)

    def third(self):
        return self.rows(4 * PATCH, 2 * PATCH)

    def fourth(self):
        return self.ref[6 * PATCH : 7 * PATCH, : PATCH + SLOT]

    def mask(self):
        value = self.rows(7 * PATCH + self.pairs * SLOT, (self.pairs + 1) * PATCH // 2)
        return jnp.concatenate([value[:, :PATCH], value[:, PATCH:]], 0)


def all_tables(blocks, columns):
    first, second, third, fourth, middle = tables()
    fourth = np.pad(fourth, ((0, 0), (0, 2 * PATCH - fourth.shape[1])))
    mask = columns_mask(blocks, columns)
    half = mask.shape[0] // 2
    return np.concatenate(
        [
            first, second, third, fourth, middle_rows(middle, columns // 2).reshape(-1, 2 * PATCH),
            np.concatenate([mask[:half], mask[half:]], 1),
        ],
        0,
    )


def passed_along(value, axis, steps):
    count = lax.axis_size(axis)
    initial, last = (max(0, -steps), min(count, count - steps))
    return lax.ppermute(value, axis, [(source, source + steps) for source in range(initial, last)])


def side_by_side(value):
    rows = value.shape[0] // 2
    return jnp.concatenate([value[:rows, :STRIDE], value[rows:, :STRIDE]], 1)


def two_terms(value):
    high = value.astype(BF16)
    return high, (value - high.astype(F32)).astype(BF16)


def only_low(value):
    low = lax.broadcasted_iota(jnp.int32, value.shape, 1) < STRIDE
    return jnp.where(low, value.astype(F32), 0.0).astype(BF16)


def parts(rows, first=0):
    step = (rows - first) // PARTS
    return [slice(top, top + step) for top in range(first, rows, step)]


def window_of(chunk, start, block):
    return jnp.concatenate([chunk(start, block), chunk(start + 1, block)], 0)


def forward(chunk, start, table, columns_of, chosen=None):
    pairs = table.pairs
    total = jnp.zeros((SLOT, 2 * PATCH), F32)
    for pair in range(pairs) if chosen is None else chosen:
        right = jnp.concatenate(
            [
                jnp.concatenate([window_of(chunk, start + w, pair + half) for half in range(2)], 1)
                for w in range(2)
            ],
            0,
        )
        left = jnp.concatenate([table.first(), table.middle(pair)], 0)
        out = lax.dot_general(left, right, (((1,), (1,)), ((), ())), preferred_element_type=F32)
        one = out[: 2 * PATCH].astype(BF16)
        for w in range(2):
            top = (2 * pair + w) * PATCH
            columns_of[top : top + PATCH, :PATCH] = one[:PATCH, w * PATCH : (w + 1) * PATCH]
            columns_of[top : top + PATCH, PATCH:] = one[PATCH:, w * PATCH : (w + 1) * PATCH]
        total += out[2 * PATCH :]
    value = total.astype(BF16)
    top = 2 * pairs * PATCH
    for w in range(2):
        columns_of[top + w * SLOT : top + (w + 1) * SLOT, :PATCH] = value[:, w * PATCH : (w + 1) * PATCH]
    columns_of[top : top + 2 * SLOT, PATCH:] = jnp.zeros((2 * SLOT, PATCH), BF16)


def energies(chunk, blocks, first_row, patch_rows, mask, sums):
    for row in range(patch_rows + 1):
        for block in range(blocks):
            pixels = chunk(first_row + row, block).astype(F32)
            sums[row : row + 1, block * PATCH : (block + 1) * PATCH] = jnp.sum(pixels * pixels, axis=0, keepdims=True)
    both = sums[0:patch_rows, :] + sums[1 : patch_rows + 1, :]
    total = sum(jnp.dot(term, mask, preferred_element_type=F32) for term in two_terms(both))
    return total * (1.0 / (PATCH * PATCH))


def prepare_kernel(upper_rows, merged, active, tile, peaks, constants, *refs):
    rows, columns = tile.shape
    patch_rows = rows // STRIDE
    height = (upper_rows + 1) * STRIDE
    first_lower = upper_rows * STRIDE
    lower = rows - first_lower
    sends = 2 if merged else 4
    outs, (whole, top, left, held), (numbers, packed, sems) = refs[:sends], refs[sends : sends + 4], refs[sends + 4 :]
    wide = columns - PATCH
    blocks = columns // PATCH

    def upwards(early, late, sem):
        return [
            pltpu.make_async_copy(tile.at[:height, :PATCH], early, sems.at[sem]),
            pltpu.make_async_copy(tile.at[:height, PATCH:], late, sems.at[sem + 1]),
        ]

    def downwards(early, late, sem):
        copies = [
            (tile.at[:STRIDE, block * PATCH : (block + 1) * PATCH], early.at[block * STRIDE : (block + 1) * STRIDE, :])
            for block in range(blocks)
        ]
        copies.append((tile.at[first_lower:, :wide], late.at[:lower, :]))
        for half in range(2):
            start = first_lower + half * lower // 2
            copies.append(
                (
                    tile.at[start : start + lower // 2, wide:],
                    late.at[lower : lower + lower // 2, half * PATCH : (half + 1) * PATCH],
                )
            )
        return [pltpu.make_async_copy(a, b, sems.at[sem + k]) for k, (a, b) in enumerate(copies)]

    def add_peaks(late):
        packed[...] = jnp.zeros_like(packed)
        for i in range(patch_rows - upper_rows):
            packed[2 * i : 2 * i + 2, : peaks.shape[2]] = numbers[upper_rows + i].astype(F32)
        late[lower + lower // 2 : lower + lower // 2 + SLOT, :PATCH] = packed[...].astype(BF16)

    fixed = [
        pltpu.make_async_copy(peaks, numbers, sems.at[0]),
        pltpu.make_async_copy(tile, whole, sems.at[1]),
        pltpu.make_async_copy(tile.at[:STRIDE, :], top, sems.at[2]),
        pltpu.make_async_copy(tile.at[:, :PATCH], left, sems.at[3]),
        pltpu.make_async_copy(constants, held, sems.at[4]),
    ]
    ups = upwards(outs[0], outs[1], 5)
    downs = downwards(outs[-2], outs[-1], 7)

    def start(copies):
        for copy in copies:
            copy.start()

    def wait(copies):
        for copy in copies:
            copy.wait()

    if merged:
        pl.when(active[1] > 0)(lambda: start(ups))
        pl.when(active[1] == 0)(lambda: start(downs))
    else:
        start(ups)
        start(downs)
    start(fixed)
    fixed[0].wait()
    if merged:
        pl.when(active[1] == 0)(lambda: add_peaks(outs[-1]))
        pl.when(active[1] > 0)(lambda: wait(ups))
        pl.when(active[1] == 0)(lambda: wait(downs))
    else:
        add_peaks(outs[-1])
        wait(ups)
        wait(downs)
    wait(fixed[1:])


def own_inner_kernel(upper_rows, active, tile, constants, spectra, once):
    rows, columns = tile.shape
    patch_rows = rows // STRIDE
    blocks = columns // PATCH
    table = Tables(constants, blocks)

    def chunk(row, block):
        return tile[row * STRIDE : (row + 1) * STRIDE, block * PATCH : (block + 1) * PATCH]

    inner = 2 * (blocks - 1) * PATCH
    for slot, (lowest, highest) in enumerate(((0, upper_rows), (upper_rows, patch_rows - 2))):

        @pl.when(active[slot] > 0)
        def _(lowest=lowest, highest=highest):
            for step in range(lowest // 2, highest // 2):
                columns_of = once.at[step % 2]
                forward(chunk, 2 * step, table, columns_of, range(blocks - 1))
                depth = columns_of.shape[0]
                for part in parts(inner) + [slice(depth - 2 * SLOT, depth)]:
                    value = jnp.dot(columns_of[part, :], table.second(), preferred_element_type=F32)
                    spectra[step, part, :] = value.astype(BF16)


def own_rest_kernel(
    upper_rows, active, tile, below, beside, constants, started, spectra, energy, strip, sums, once
):
    rows, columns = tile.shape
    patch_rows = rows // STRIDE
    blocks = columns // PATCH
    table = Tables(constants, blocks)
    strip[...] = only_low(beside[...])

    def chunk(row, block):
        at = slice(row * STRIDE, (row + 1) * STRIDE)
        if block == blocks:
            return strip[at, :]
        lanes = slice(block * PATCH, (block + 1) * PATCH)
        return tile[at, lanes] if row < patch_rows else below[:, lanes]

    inner = 2 * (blocks - 1) * PATCH
    for slot, (lowest, highest) in enumerate(((0, upper_rows), (upper_rows, patch_rows))):

        @pl.when(active[slot] > 0)
        def _(slot=slot, lowest=lowest, highest=highest):
            for step in range(lowest // 2, highest // 2):
                columns_of = once.at[step % 2]
                depth = columns_of.shape[0]
                last = step == patch_rows // 2 - 1
                forward(chunk, 2 * step, table, columns_of, None if last else [blocks - 1])
                for part in parts(depth, 0 if last else inner):
                    value = jnp.dot(columns_of[part, :], table.second(), preferred_element_type=F32)
                    middle = max(part.start, depth - 2 * SLOT)
                    if last or part.stop <= middle:
                        spectra[step, part, :] = value.astype(BF16)
                    else:
                        size = part.stop - middle
                        spectra[step, part.start : middle, :] = value[:-size].astype(BF16)
                        before = spectra[step, middle : part.stop, :].astype(F32)
                        spectra[step, middle : part.stop, :] = (before + value[-size:]).astype(BF16)
            energy[slot, : highest - lowest, :] = energies(
                chunk, blocks + 1, lowest, highest - lowest, table.mask(), sums
            )


def crossed(own, other, flipped):
    own = own.astype(F32)
    own_re, own_im = own[:, :PATCH], own[:, PATCH:]
    re, im = other[:, :PATCH], other[:, PATCH:]
    real = own_re * re + own_im * im
    imaginary = own_im * re - own_re * im if flipped else own_re * im - own_im * re
    return jnp.concatenate([real.astype(BF16), imaginary.astype(BF16)], 1)


def pair_kernel(
    slot, first_row, patch_rows, patch_columns, active, peaks, early, late, beside, spectra, energy,
    constants, out, strip, sums, once, crosses, inverse, peak, moments, offsets,
    *surfaces
):
    flipped = slot == 1
    size = patch_rows * SLOT
    pairs = patch_columns // 2
    blocks = pairs
    table = Tables(constants, pairs)

    @pl.when(active[slot] == 0)
    def _():
        out[...] = jnp.zeros_like(out)

    @pl.when(active[slot] > 0)
    def _():
        if flipped:
            half = strip.shape[0] // 2
            packed = beside[...].astype(F32)
            low = lax.broadcasted_iota(jnp.int32, packed.shape, 1) < STRIDE
            strip[:half, :] = jnp.where(low, packed, 0.0).astype(BF16)
            strip[half:, :] = jnp.where(low, pltpu.roll(packed, STRIDE, 1), 0.0).astype(BF16)
        else:
            packed = beside[: strip.shape[0], :].astype(F32)
            strip[...] = only_low(pltpu.roll(packed, STRIDE, 1))

        def chunk(row, block):
            at = slice(row * STRIDE, (row + 1) * STRIDE)
            if block == blocks:
                return strip[at, :]
            if not flipped:
                return early[at, :] if block == 0 else late[at, (block - 1) * PATCH : block * PATCH]
            if row == patch_rows:
                return early[block * STRIDE : (block + 1) * STRIDE, :]
            if block < blocks - 1:
                return late[at, block * PATCH : (block + 1) * PATCH]
            side, place = divmod(row, patch_rows // 2)
            top = (patch_rows + place) * STRIDE
            return late[top : top + STRIDE, side * PATCH : (side + 1) * PATCH]

        row_of = lax.broadcasted_iota(jnp.int32, (SLOT, 2 * PATCH), 0)
        for step in range(patch_rows // 2):
            columns_of, cross, back = once.at[step % 2], crosses.at[step % 2], inverse.at[step % 2]
            forward(chunk, 2 * step, table, columns_of)
            for part in parts(columns_of.shape[0]):
                spectrum = jnp.dot(columns_of[part, :], table.second(), preferred_element_type=F32)
                cross[part, :] = crossed(spectra[step + first_row // 2, part, :], spectrum, flipped)
            for part in parts(columns_of.shape[0]):
                back[part, :] = jnp.dot(cross[part, :], table.third(), preferred_element_type=F32).astype(BF16)
            top = 2 * pairs * PATCH
            mid = back[top : top + 2 * SLOT, :PATCH].astype(F32)
            mid = jnp.concatenate([mid[:SLOT], mid[SLOT:]], 1)
            for column in range(patch_columns):
                a = (column // 2) * 2 * PATCH + (column % 2) * HALF
                b = a + PATCH
                right = jnp.concatenate(
                    [
                        jnp.concatenate([back[a : a + HALF, :PATCH], back[b : b + HALF, :PATCH]], 1),
                        jnp.concatenate([back[a : a + HALF, PATCH:], back[b : b + HALF, PATCH:]], 1),
                        jnp.where(row_of == column, mid, 0.0).astype(BF16),
                    ],
                    0,
                )
                value = jnp.dot(table.fourth(), right, preferred_element_type=F32)
                largest = jnp.max(jnp.abs(value), axis=0, keepdims=True)
                for which in range(2):
                    lanes = slice(which * PATCH, (which + 1) * PATCH)
                    i = 2 * step + which
                    at = i * SLOT + column
                    surface = surfaces[2 * column + which]
                    surface[EDGE : EDGE + PATCH, :] = value[:, lanes]
                    surface[:EDGE, :] = value[PATCH - EDGE :, lanes]
                    surface[EDGE + PATCH :, :] = value[:EDGE, lanes]
                    peak[at : at + 1, :] = largest[:, lanes]
                    along = peaks[i, 1, column] + (EDGE - WIN // 2)
                    moments[at * 8 : at * 8 + 8, :] = surface[pl.ds(along, 8), :]
                    offsets[at : at + 1, :] = jnp.full((1, PATCH), peaks[i, 0, column], jnp.int32)
        other = energies(chunk, blocks + 1, 0, patch_rows, table.mask(), sums)
        scales = float(PATCH) ** 3 * jnp.sqrt((energy[slot, :patch_rows, :] + 1e-05) * (other + 1e-05))

        lane = lax.broadcasted_iota(jnp.int32, (1, PATCH), 1)
        scale = jnp.ones((1, PATCH), F32)
        for i in range(patch_rows):
            row = scales[i : i + 1, :]
            row = pltpu.roll(row, i * SLOT, 1) if i else row
            scale = jnp.where((lane >= i * SLOT) & (lane < i * SLOT + patch_columns), row, scale)
        peak_rows = peak[...]
        height = jnp.max(jnp.transpose(peak_rows), axis=0, keepdims=True) / scale + 1e-05

        lane = lax.broadcasted_iota(jnp.int32, (size, PATCH), 1)
        offset = (lane - offsets[...] + (WIN // 2 + PATCH)) & (PATCH - 1)
        u = (offset - WIN // 2).astype(F32)
        within = offset < WIN
        numbers = np.arange(WIN) - WIN // 2
        middle_square = float(np.mean(numbers**2))
        u0 = jnp.where(within, 1.0, 0.0)
        u1 = jnp.where(within, u, 0.0)
        u2 = jnp.where(within, u * u - middle_square, 0.0)
        v0 = v1 = v2 = jnp.zeros((size, PATCH), F32)
        for v in range(WIN):
            value = moments[pl.ds(v, size, stride=8), :]
            position = float(v - WIN // 2)
            v0 += value
            v1 += position * value
            v2 += (position * position - middle_square) * value
        factors = ((u0, v0), (u1, v0), (u0, v1), (u2, v0), (u0, v2), (u1, v1))
        terms = [two_terms(fu * fv) for fu, fv in factors]
        which_e = lax.broadcasted_iota(jnp.int32, (SLOT, len(terms) * PATCH), 0)
        of_lane = lax.broadcasted_iota(jnp.int32, (SLOT, len(terms) * PATCH), 1)
        ones = jnp.where((of_lane >= which_e * PATCH) & (of_lane < (which_e + 1) * PATCH), 1.0, 0.0).astype(BF16)
        total = sum(
            lax.dot_general(
                ones, jnp.concatenate([t[k] for t in terms], 1), (((1,), (1,)), ((), ())), preferred_element_type=F32
            )
            for k in range(2)
        )[:8]
        linear = float(np.sum(numbers**2))
        quadratic = float(np.sum((numbers**2 - middle_square) ** 2))
        norms = (
            float(WIN), math.sqrt(WIN * linear), math.sqrt(WIN * linear), math.sqrt(WIN * quadratic),
            math.sqrt(WIN * quadratic), linear,
        )
        e_row = lax.broadcasted_iota(jnp.int32, (8, size), 0)
        factor = jnp.zeros((8, size), F32)
        for e, norm in enumerate(norms):
            factor = jnp.where(e_row == e, 1.0 / norm, factor)
        out[:, :size] = total * factor / (scale * height)[:, :size]
        if size < PATCH:
            out[:, size:] = jnp.zeros((8, PATCH - size), F32)


def join_kernel(upper_rows, upper, lower, valid, out):
    count, patch_rows, _, patch_columns = out.shape
    for i in range(patch_rows):
        source, at = (upper, i) if i < upper_rows else (lower, i - upper_rows)
        value = source[...]
        turned = pltpu.roll(value, PATCH - at * SLOT, 1) if at else value
        keep = valid[i].astype(F32)
        for e in range(count):
            out[e, i] = turned[e : e + 1, :patch_columns] * keep


def body(sections, peaks, valid):
    tile = sections[0]
    rows, columns = tile.shape
    patch_rows, patch_columns = rows // STRIDE, columns // STRIDE
    pairs = patch_columns // 2
    upper_rows = (patch_rows // 2 + 1) // 2 * 2
    lower_rows = patch_rows - upper_rows
    first_lower = upper_rows * STRIDE
    upper_height = first_lower + STRIDE
    lower_height = lower_rows * STRIDE + STRIDE
    count, height = lax.axis_size("gz"), lax.axis_size("gy")
    position = lax.axis_index("gz")
    active = jnp.stack([position < count - 1, position > 0]).astype(jnp.int32)
    peaks = jnp.transpose(peaks, (0, 2, 1, 3))[0]
    valid = jnp.transpose(valid, (1, 0, 2))

    constants = jnp.asarray(all_tables(columns // PATCH + 1, patch_columns), BF16)

    vmem = pl.BlockSpec(memory_space=pltpu.VMEM)
    smem = pl.BlockSpec(memory_space=pltpu.SMEM)

    def grant(mib):
        return pltpu.CompilerParams(vmem_limit_bytes=mib << 20)

    def shape(*dims, dtype=BF16):
        return jax.ShapeDtypeStruct(dims, dtype)

    merged = count == 2
    early, late = shape(upper_height, PATCH), shape(upper_height, columns - PATCH)
    anywhere = pl.BlockSpec(memory_space=pltpu.HBM)
    outs = pl.pallas_call(
        functools.partial(prepare_kernel, upper_rows, merged),
        out_shape=((early, late) if merged else (early, late) * 2)
        + (shape(rows, columns), shape(STRIDE, columns), shape(rows, PATCH), shape(*constants.shape)),
        in_specs=[smem] + [anywhere] * 3,
        out_specs=(vmem,) * (6 if merged else 8),
        scratch_shapes=[
            pltpu.VMEM(peaks.shape, jnp.int32),
            pltpu.VMEM((SLOT, PATCH), F32),
            pltpu.SemaphoreType.DMA((7 + columns // PATCH + 3,)),
        ],
        compiler_params=grant(1),
        name="prepare",
    )(active, *(pltpu.with_memory_space_constraint(x, pltpu.HBM) for x in (tile, peaks, constants)))
    tile, top, left, constants = outs[-4:]

    up = [((s + 1) * height + y, s * height + y) for s in range(count - 1) for y in range(height)]
    down = [(s * height + y + 1, (s + 1) * height + y) for s in range(count - 1) for y in range(height - 1)]
    if merged:
        early_upper = early_lower = lax.ppermute(outs[0], ("gz", "gy"), up + down)
        late_upper = late_lower = lax.ppermute(outs[1], "gz", [(0, 1), (1, 0)])
    else:
        early_upper = lax.ppermute(outs[0], ("gz", "gy"), up)
        early_lower = lax.ppermute(outs[2], ("gz", "gy"), down)
        late_upper = passed_along(outs[1], "gz", -1)
        late_lower = passed_along(outs[3], "gz", 1)
    below = passed_along(top, "gy", -1)
    others = jnp.pad(early_upper[:, :STRIDE], ((0, rows + STRIDE - upper_height), (0, 0)))
    ours = jnp.concatenate([left[:, :STRIDE], below[:, :STRIDE]], 0)
    beside = passed_along(jnp.concatenate([ours, others], 1), "gx", -1)
    edge_lower = passed_along(side_by_side(beside[first_lower : rows + STRIDE]), "gz", 1)

    steps = patch_rows // 2
    depth = 2 * pairs * PATCH + 2 * SLOT
    width = columns + PATCH
    own_cost = pl.CostEstimate(flops=2_000_000_000, bytes_accessed=6_000_000, transcendentals=0)
    own_inner = pl.pallas_call(
        functools.partial(own_inner_kernel, upper_rows),
        out_shape=shape(steps, depth, 2 * PATCH),
        in_specs=[smem] + [vmem] * 2,
        out_specs=vmem,
        scratch_shapes=[pltpu.VMEM((2, depth, 2 * PATCH), BF16)],
        compiler_params=grant(6),
        cost_estimate=own_cost,
        name="own_inner",
    )
    spectra = own_inner(active, tile, constants)
    own_rest = pl.pallas_call(
        functools.partial(own_rest_kernel, upper_rows),
        out_shape=(shape(steps, depth, 2 * PATCH), shape(2, 8, PATCH, dtype=F32)),
        in_specs=[smem] + [vmem] * 5,
        out_specs=(vmem, vmem),
        scratch_shapes=[
            pltpu.VMEM((rows + STRIDE, PATCH), BF16),
            pltpu.VMEM((8, width), F32),
            pltpu.VMEM((2, depth, 2 * PATCH), BF16),
        ],
        input_output_aliases={5: 0},
        compiler_params=grant(6),
        cost_estimate=own_cost,
        name="own_rest",
    )
    spectra, energy = own_rest(active, tile, below, beside, constants, spectra)

    def correlated(slot, first_row, count_rows, strip_rows, peaks_here, early, late, beside):
        size = count_rows * SLOT
        return pl.pallas_call(
            functools.partial(pair_kernel, slot, first_row, count_rows, patch_columns),
            out_shape=shape(8, PATCH, dtype=F32),
            in_specs=[smem, smem] + [vmem] * 6,
            out_specs=vmem,
            scratch_shapes=[
                pltpu.VMEM((strip_rows, PATCH), BF16),
                pltpu.VMEM((8, width), F32),
                pltpu.VMEM((2, depth, 2 * PATCH), BF16),
                pltpu.VMEM((2, depth, 2 * PATCH), BF16),
                pltpu.VMEM((2, depth, 2 * PATCH), BF16),
                pltpu.VMEM((PATCH, PATCH), F32),
                pltpu.VMEM((size * 8, PATCH), F32),
                pltpu.VMEM((size, PATCH), jnp.int32),
            ]
            + [pltpu.VMEM((PATCH + 2 * EDGE, PATCH), F32)] * (2 * patch_columns),
            compiler_params=grant(12),
            cost_estimate=pl.CostEstimate(flops=4_000_000_000, bytes_accessed=6_000_000, transcendentals=0),
        )(active, peaks_here, early, late, beside, spectra, energy, constants)

    at = lower_rows * STRIDE + lower_rows * STRIDE // 2
    peaks_lower = late_lower[at : at + 2 * lower_rows, :patch_columns].astype(jnp.int32)
    peaks_lower = peaks_lower.reshape(lower_rows, 2, patch_columns)
    lower = correlated(1, upper_rows, lower_rows, lower_height, peaks_lower, early_lower, late_lower, edge_lower)
    lower = passed_along(lower, "gz", -1)
    upper = correlated(0, 0, upper_rows, upper_height, peaks, early_upper, late_upper, beside)
    fit = pl.pallas_call(
        functools.partial(join_kernel, upper_rows),
        out_shape=shape(6, patch_rows, 1, patch_columns, dtype=F32),
        in_specs=[vmem] * 3,
        out_specs=vmem,
        compiler_params=grant(1),
        name="join",
    )(upper, lower, valid)
    return jnp.transpose(fit, (2, 0, 1, 3))


def solution(mesh):
    in_specs = (P("gz", "gy", "gx"), P("gz", None, "gy", "gx"), P("gz", "gy", "gx"))
    out_specs = P("gz", None, "gy", "gx")
    return jax.shard_map(body, mesh=mesh, in_specs=in_specs, out_specs=out_specs, check_vma=False)
```

```python
import functools
import math

import jax
import jax.numpy as jnp
import numpy as np
from jax import lax
from jax.experimental import pallas as pl
from jax.experimental.pallas import tpu as pltpu
from jax.sharding import PartitionSpec as P


PATCH = 128
STRIDE = 64
WIN = 5
HALF = PATCH // 2
EDGE = 8
SLOT = 16
PARTS = 2
F32 = jnp.float32
BF16 = jnp.bfloat16


def tables():
    index = np.arange(PATCH)
    phase = (index[:, None] * index[None, :] % PATCH).astype(np.float64) * (2.0 * math.pi / PATCH)
    cosine = np.asarray(np.cos(phase), dtype=jnp.bfloat16).astype(np.float32)
    sine = np.asarray(np.sin(phase), dtype=jnp.bfloat16).astype(np.float32)
    first = np.zeros((4 * HALF, 2 * PATCH), np.float32)
    for part, table in enumerate((cosine, -sine)):
        for which in range(2):
            top = part * PATCH + which * HALF
            first[top : top + HALF, which * STRIDE : which * STRIDE + PATCH] = table[:HALF]
    second = np.block([[cosine, -sine], [sine, cosine]])
    third = np.block([[cosine, sine], [-sine, cosine]])
    weight = np.where(np.arange(HALF) == 0, 1.0, 2.0)[None, :]
    fourth = np.concatenate(
        [cosine[:, :HALF] * weight, -sine[:, :HALF] * weight, np.repeat(cosine[:, HALF : HALF + 1], SLOT, 1)], 1
    )
    return first, second, third, fourth, cosine[HALF]


def middle_rows(middle, pairs):
    rows = np.zeros((pairs, SLOT, 2 * PATCH), np.float32)
    for pair in range(pairs):
        for which in range(2):
            rows[pair, 2 * pair + which, which * STRIDE : which * STRIDE + PATCH] = middle
    return rows


def columns_mask(blocks, columns):
    mask = np.zeros((blocks * PATCH, PATCH), np.float32)
    for column in range(columns):
        mask[column * STRIDE : column * STRIDE + PATCH, column] = 1.0
    return mask


class Tables:
    def __init__(self, ref, pairs):
        self.ref, self.pairs = ref, pairs

    def rows(self, top, count):
        return self.ref[top : top + count, :]

    def first(self):
        return self.rows(0, 2 * PATCH)

    def middle(self, pair):
        return self.rows(6 * PATCH + PATCH + pair * SLOT, SLOT)

    def second(self):
        return self.rows(2 * PATCH, 2 * PATCH)

    def third(self):
        return self.rows(4 * PATCH, 2 * PATCH)

    def fourth(self):
        return self.ref[6 * PATCH : 7 * PATCH, : PATCH + SLOT]

    def mask(self):
        value = self.rows(7 * PATCH + self.pairs * SLOT, (self.pairs + 1) * PATCH // 2)
        return jnp.concatenate([value[:, :PATCH], value[:, PATCH:]], 0)


def all_tables(blocks, columns):
    first, second, third, fourth, middle = tables()
    fourth = np.pad(fourth, ((0, 0), (0, 2 * PATCH - fourth.shape[1])))
    mask = columns_mask(blocks, columns)
    half = mask.shape[0] // 2
    return np.concatenate(
        [
            first, second, third, fourth, middle_rows(middle, columns // 2).reshape(-1, 2 * PATCH),
            np.concatenate([mask[:half], mask[half:]], 1),
        ],
        0,
    )


def passed_along(value, axis, steps):
    count = lax.axis_size(axis)
    initial, last = (max(0, -steps), min(count, count - steps))
    return lax.ppermute(value, axis, [(source, source + steps) for source in range(initial, last)])


def side_by_side(value):
    rows = value.shape[0] // 2
    return jnp.concatenate([value[:rows, :STRIDE], value[rows:, :STRIDE]], 1)


def two_terms(value):
    high = value.astype(BF16)
    return high, (value - high.astype(F32)).astype(BF16)


def only_low(value):
    low = lax.broadcasted_iota(jnp.int32, value.shape, 1) < STRIDE
    return jnp.where(low, value.astype(F32), 0.0).astype(BF16)


def working(count):
    position = lax.axis_index("gz")
    return position < count - 1, position > 0


def start_all(copies):
    for copy in copies:
        copy.start()


def wait_all(copies):
    for copy in copies:
        copy.wait()


def parts(rows, first=0):
    step = (rows - first) // PARTS
    return [slice(top, top + step) for top in range(first, rows, step)]


def window_of(chunk, start, block):
    return jnp.concatenate([chunk(start, block), chunk(start + 1, block)], 0)


def forward(chunk, start, table, columns_of, chosen=None):
    pairs = table.pairs
    total = jnp.zeros((SLOT, 2 * PATCH), F32)
    for pair in range(pairs) if chosen is None else chosen:
        right = jnp.concatenate(
            [
                jnp.concatenate([window_of(chunk, start + w, pair + half) for half in range(2)], 1)
                for w in range(2)
            ],
            0,
        )
        left = jnp.concatenate([table.first(), table.middle(pair)], 0)
        out = lax.dot_general(left, right, (((1,), (1,)), ((), ())), preferred_element_type=F32)
        one = out[: 2 * PATCH].astype(BF16)
        for w in range(2):
            top = (2 * pair + w) * PATCH
            columns_of[top : top + PATCH, :PATCH] = one[:PATCH, w * PATCH : (w + 1) * PATCH]
            columns_of[top : top + PATCH, PATCH:] = one[PATCH:, w * PATCH : (w + 1) * PATCH]
        total += out[2 * PATCH :]
    value = total.astype(BF16)
    top = 2 * pairs * PATCH
    for w in range(2):
        columns_of[top + w * SLOT : top + (w + 1) * SLOT, :PATCH] = value[:, w * PATCH : (w + 1) * PATCH]
    columns_of[top : top + 2 * SLOT, PATCH:] = jnp.zeros((2 * SLOT, PATCH), BF16)


def energies(chunk, blocks, first_row, patch_rows, mask, sums):
    for row in range(patch_rows + 1):
        for block in blocks:
            pixels = chunk(first_row + row, block).astype(F32)
            sums[row : row + 1, block * PATCH : (block + 1) * PATCH] = jnp.sum(pixels * pixels, axis=0, keepdims=True)
    lanes = slice(blocks[0] * PATCH, (blocks[-1] + 1) * PATCH)
    both = sums[0:patch_rows, lanes] + sums[1 : patch_rows + 1, lanes]
    total = sum(jnp.dot(term, mask[lanes], preferred_element_type=F32) for term in two_terms(both))
    return total * (1.0 / (PATCH * PATCH))


def prepare_kernel(upper_rows, merged, count, tile, peaks, *refs):
    rows, columns = tile.shape
    patch_rows = rows // STRIDE
    height = (upper_rows + 1) * STRIDE
    first_lower = upper_rows * STRIDE
    lower = rows - first_lower
    sends = 3 if merged else 5
    outs, (top, left), (numbers, packed, sems) = refs[:sends], refs[sends : sends + 2], refs[sends + 2 :]
    up, down = outs[:3], outs[:2] if merged else outs[3:]
    blocks = columns // PATCH
    inside = blocks - 2
    _, has_before = working(count)

    def lanes(block):
        return slice(block * PATCH, (block + 1) * PATCH)

    upwards = [
        (tile.at[:height, lanes(0)], up[0]),
        (tile.at[:height, PATCH : PATCH * (blocks - 1)], up[1]),
        (tile.at[:height, lanes(blocks - 1)], up[2]),
    ]
    early, late = down
    tall = height - lower
    downwards = [(tile.at[:STRIDE, lanes(b)], early.at[b * STRIDE : (b + 1) * STRIDE, :]) for b in range(blocks)]
    downwards.append((tile.at[first_lower:, : inside * PATCH], late.at[:lower, :]))
    for k in range(2):
        source = lanes(inside + k)
        downwards.append((tile.at[first_lower : first_lower + tall, source], late.at[lower:, lanes(k)]))
        at = lower + k * (lower - tall)
        downwards.append((tile.at[first_lower + tall :, source], late.at[at : at + lower - tall, lanes(2)]))
    peaks_at = lower + 2 * (lower - tall)

    def add_peaks():
        packed[...] = jnp.zeros_like(packed)
        for i in range(patch_rows - upper_rows):
            packed[2 * i : 2 * i + 2, : peaks.shape[2]] = numbers[upper_rows + i].astype(F32)
        late[peaks_at : peaks_at + SLOT, lanes(2)] = packed[...].astype(BF16)

    fixed = [(peaks, numbers), (tile.at[:STRIDE, :], top), (tile.at[:, :PATCH], left)]
    groups = []
    used = 0
    for group in (upwards, downwards, fixed):
        groups.append([pltpu.make_async_copy(a, b, sems.at[used + k]) for k, (a, b) in enumerate(group)])
        used += len(group)
    upwards, downwards, fixed = groups
    if merged:
        pl.when(has_before)(lambda: start_all(upwards))
        pl.when(jnp.logical_not(has_before))(lambda: start_all(downwards))
        start_all(fixed)
        fixed[0].wait()
        pl.when(jnp.logical_not(has_before))(add_peaks)
        pl.when(has_before)(lambda: wait_all(upwards))
        pl.when(jnp.logical_not(has_before))(lambda: wait_all(downwards))
        wait_all(fixed[1:])
    else:
        start_all(fixed + upwards + downwards)
        fixed[0].wait()
        add_peaks()
        wait_all(fixed[1:] + upwards + downwards)


def own_inner_kernel(upper_rows, count, source, tables_source, spectra, tile, constants, once, sems):
    rows, columns = tile.shape
    patch_rows = rows // STRIDE
    blocks = columns // PATCH
    table = Tables(constants, blocks)

    def chunk(row, block):
        return tile[row * STRIDE : (row + 1) * STRIDE, block * PATCH : (block + 1) * PATCH]

    copies = [
        pltpu.make_async_copy(source, tile, sems.at[0]),
        pltpu.make_async_copy(tables_source, constants, sems.at[1]),
    ]
    start_all(copies)
    wait_all(copies)
    active = working(count)
    inner = 2 * (blocks - 1) * PATCH
    for slot, (lowest, highest) in enumerate(((0, upper_rows), (upper_rows, patch_rows - 2))):

        @pl.when(active[slot])
        def _(lowest=lowest, highest=highest):
            for step in range(lowest // 2, highest // 2):
                columns_of = once.at[step % 2]
                forward(chunk, 2 * step, table, columns_of, range(blocks - 1))
                depth = columns_of.shape[0]
                for part in parts(inner) + [slice(depth - 2 * SLOT, depth)]:
                    value = jnp.dot(columns_of[part, :], table.second(), preferred_element_type=F32)
                    spectra[step, part, :] = value.astype(BF16)


def own_rest_kernel(
    upper_rows, count, tile, below, beside, constants, started, spectra, energy, strip, sums, once
):
    rows, columns = tile.shape
    patch_rows = rows // STRIDE
    blocks = columns // PATCH
    table = Tables(constants, blocks)
    strip[...] = only_low(beside[...])
    active = working(count)

    def chunk(row, block):
        at = slice(row * STRIDE, (row + 1) * STRIDE)
        if block == blocks:
            return strip[at, :]
        lanes = slice(block * PATCH, (block + 1) * PATCH)
        return tile[at, lanes] if row < patch_rows else below[:, lanes]

    inner = 2 * (blocks - 1) * PATCH
    for slot, (lowest, highest) in enumerate(((0, upper_rows), (upper_rows, patch_rows))):

        @pl.when(active[slot])
        def _(slot=slot, lowest=lowest, highest=highest):
            for step in range(lowest // 2, highest // 2):
                columns_of = once.at[step % 2]
                depth = columns_of.shape[0]
                last = step == patch_rows // 2 - 1
                forward(chunk, 2 * step, table, columns_of, None if last else [blocks - 1])
                for part in parts(depth, 0 if last else inner):
                    value = jnp.dot(columns_of[part, :], table.second(), preferred_element_type=F32)
                    middle = max(part.start, depth - 2 * SLOT)
                    if last or part.stop <= middle:
                        spectra[step, part, :] = value.astype(BF16)
                    else:
                        size = part.stop - middle
                        spectra[step, part.start : middle, :] = value[:-size].astype(BF16)
                        before = spectra[step, middle : part.stop, :].astype(F32)
                        spectra[step, middle : part.stop, :] = (before + value[-size:]).astype(BF16)
            energy[slot, : highest - lowest, :] = energies(
                chunk, range(blocks + 1), lowest, highest - lowest, table.mask(), sums
            )


def crossed(own, other, flipped):
    own = own.astype(F32)
    own_re, own_im = own[:, :PATCH], own[:, PATCH:]
    re, im = other[:, :PATCH], other[:, PATCH:]
    real = own_re * re + own_im * im
    imaginary = own_im * re - own_re * im if flipped else own_re * im - own_im * re
    return jnp.concatenate([real.astype(BF16), imaginary.astype(BF16)], 1)


def pair_kernel(
    slot, chosen, first_row, patch_rows, patch_columns, count, peaks_source, early, late, last, beside, spectra, energy,
    constants, out, peaks, sem, strip, sums, once, crosses, inverse, peak, moments, offsets, *surfaces
):
    flipped = slot == 1
    size = patch_rows * SLOT
    pairs = patch_columns // 2
    blocks = pairs
    table = Tables(constants, pairs)
    active = working(count)[slot]
    patches = range(2 * chosen[0], 2 * chosen[-1] + 2)

    @pl.when(jnp.logical_not(active))
    def _():
        out[...] = jnp.zeros_like(out)

    @pl.when(active)
    def _():
        fetch = pltpu.make_async_copy(peaks_source.at[:patch_rows], peaks, sem)
        fetch.start()
        if chosen[-1] == pairs - 1:
            if flipped:
                half = strip.shape[0] // 2
                packed = beside[...].astype(F32)
                low = lax.broadcasted_iota(jnp.int32, packed.shape, 1) < STRIDE
                strip[:half, :] = jnp.where(low, packed, 0.0).astype(BF16)
                strip[half:, :] = jnp.where(low, pltpu.roll(packed, STRIDE, 1), 0.0).astype(BF16)
            else:
                packed = beside[: strip.shape[0], :].astype(F32)
                strip[...] = only_low(pltpu.roll(packed, STRIDE, 1))

        def lanes_of(block):
            return slice(block * PATCH, (block + 1) * PATCH)

        def chunk(row, block):
            at = slice(row * STRIDE, (row + 1) * STRIDE)
            if block == blocks:
                return strip[at, :]
            if not flipped:
                if block == 0:
                    return early[at, :]
                return last[at, :] if block == blocks - 1 else late[at, lanes_of(block - 1)]
            if row == patch_rows:
                return early[block * STRIDE : (block + 1) * STRIDE, :]
            inside = blocks - 2
            if block < inside:
                return late[at, lanes_of(block)]
            lower = patch_rows * STRIDE
            tall = late.shape[0] - lower
            start = row * STRIDE
            if start < tall:
                return late[lower + start : lower + start + STRIDE, lanes_of(block - inside)]
            start += lower + (block - inside) * (lower - tall) - tall
            return late[start : start + STRIDE, lanes_of(2)]

        row_of = lax.broadcasted_iota(jnp.int32, (SLOT, 2 * PATCH), 0)
        for step in range(patch_rows // 2):
            columns_of, cross, back = once.at[step % 2], crosses.at[step % 2], inverse.at[step % 2]
            forward(chunk, 2 * step, table, columns_of, chosen)
            depth = columns_of.shape[0]
            if len(chosen) == pairs:
                rows = parts(depth)
            else:
                rows = parts(patches.stop * PATCH, patches.start * PATCH) + [slice(depth - 2 * SLOT, depth)]
            for part in rows:
                spectrum = jnp.dot(columns_of[part, :], table.second(), preferred_element_type=F32)
                cross[part, :] = crossed(spectra[step + first_row // 2, part, :], spectrum, flipped)
            for part in rows:
                back[part, :] = jnp.dot(cross[part, :], table.third(), preferred_element_type=F32).astype(BF16)
            top = 2 * pairs * PATCH
            mid = back[top : top + 2 * SLOT, :PATCH].astype(F32)
            mid = jnp.concatenate([mid[:SLOT], mid[SLOT:]], 1)
            if step == 0:
                fetch.wait()
            for column in patches:
                a = (column // 2) * 2 * PATCH + (column % 2) * HALF
                b = a + PATCH
                right = jnp.concatenate(
                    [
                        jnp.concatenate([back[a : a + HALF, :PATCH], back[b : b + HALF, :PATCH]], 1),
                        jnp.concatenate([back[a : a + HALF, PATCH:], back[b : b + HALF, PATCH:]], 1),
                        jnp.where(row_of == column, mid, 0.0).astype(BF16),
                    ],
                    0,
                )
                value = jnp.dot(table.fourth(), right, preferred_element_type=F32)
                largest = jnp.max(jnp.abs(value), axis=0, keepdims=True)
                for which in range(2):
                    lanes = slice(which * PATCH, (which + 1) * PATCH)
                    i = 2 * step + which
                    at = i * SLOT + column
                    surface = surfaces[2 * (column - patches.start) + which]
                    surface[EDGE : EDGE + PATCH, :] = value[:, lanes]
                    surface[:EDGE, :] = value[PATCH - EDGE :, lanes]
                    surface[EDGE + PATCH :, :] = value[:EDGE, lanes]
                    peak[at : at + 1, :] = largest[:, lanes]
                    along = peaks[i, 1, column] + (EDGE - WIN // 2)
                    moments[at * 8 : at * 8 + 8, :] = surface[pl.ds(along, 8), :]
                    offsets[at : at + 1, :] = jnp.full((1, PATCH), peaks[i, 0, column], jnp.int32)
        other = energies(chunk, range(chosen[0], chosen[-1] + 2), 0, patch_rows, table.mask(), sums)
        scales = float(PATCH) ** 3 * jnp.sqrt((energy[slot, :patch_rows, :] + 1e-05) * (other + 1e-05))

        lane = lax.broadcasted_iota(jnp.int32, (1, PATCH), 1)
        scale = jnp.ones((1, PATCH), F32)
        for i in range(patch_rows):
            row = scales[i : i + 1, :]
            row = pltpu.roll(row, i * SLOT, 1) if i else row
            scale = jnp.where((lane >= i * SLOT + patches.start) & (lane < i * SLOT + patches.stop), row, scale)
        peak_rows = peak[...]
        height = jnp.max(jnp.transpose(peak_rows), axis=0, keepdims=True) / scale + 1e-05

        lane = lax.broadcasted_iota(jnp.int32, (size, PATCH), 1)
        offset = (lane - offsets[...] + (WIN // 2 + PATCH)) & (PATCH - 1)
        u = (offset - WIN // 2).astype(F32)
        within = offset < WIN
        numbers = np.arange(WIN) - WIN // 2
        middle_square = float(np.mean(numbers**2))
        u0 = jnp.where(within, 1.0, 0.0)
        u1 = jnp.where(within, u, 0.0)
        u2 = jnp.where(within, u * u - middle_square, 0.0)
        v0 = v1 = v2 = jnp.zeros((size, PATCH), F32)
        for v in range(WIN):
            value = moments[pl.ds(v, size, stride=8), :]
            position = float(v - WIN // 2)
            v0 += value
            v1 += position * value
            v2 += (position * position - middle_square) * value
        factors = ((u0, v0), (u1, v0), (u0, v1), (u2, v0), (u0, v2), (u1, v1))
        terms = [two_terms(fu * fv) for fu, fv in factors]
        which_e = lax.broadcasted_iota(jnp.int32, (SLOT, len(terms) * PATCH), 0)
        of_lane = lax.broadcasted_iota(jnp.int32, (SLOT, len(terms) * PATCH), 1)
        ones = jnp.where((of_lane >= which_e * PATCH) & (of_lane < (which_e + 1) * PATCH), 1.0, 0.0).astype(BF16)
        total = sum(
            lax.dot_general(
                ones, jnp.concatenate([t[k] for t in terms], 1), (((1,), (1,)), ((), ())), preferred_element_type=F32
            )
            for k in range(2)
        )[:8]
        linear = float(np.sum(numbers**2))
        quadratic = float(np.sum((numbers**2 - middle_square) ** 2))
        norms = (
            float(WIN), math.sqrt(WIN * linear), math.sqrt(WIN * linear), math.sqrt(WIN * quadratic),
            math.sqrt(WIN * quadratic), linear,
        )
        e_row = lax.broadcasted_iota(jnp.int32, (8, size), 0)
        factor = jnp.zeros((8, size), F32)
        for e, norm in enumerate(norms):
            factor = jnp.where(e_row == e, 1.0 / norm, factor)
        out[:, :size] = total * factor / (scale * height)[:, :size]
        if size < PATCH:
            out[:, size:] = jnp.zeros((8, PATCH - size), F32)


def join_kernel(upper_rows, split, upper_left, upper_right, lower, valid, out):
    count, patch_rows, _, patch_columns = out.shape
    lane = lax.broadcasted_iota(jnp.int32, upper_left.shape, 1) & (SLOT - 1)
    upper = jnp.where(lane < split, upper_left[...], upper_right[...])
    for i in range(patch_rows):
        value, at = (upper, i) if i < upper_rows else (lower[...], i - upper_rows)
        turned = pltpu.roll(value, PATCH - at * SLOT, 1) if at else value
        keep = valid[i].astype(F32)
        for e in range(count):
            out[e, i] = turned[e : e + 1, :patch_columns] * keep


def body(sections, peaks, valid):
    tile = sections[0]
    rows, columns = tile.shape
    patch_rows, patch_columns = rows // STRIDE, columns // STRIDE
    pairs = patch_columns // 2
    upper_rows = (patch_rows // 2 + 1) // 2 * 2
    lower_rows = patch_rows - upper_rows
    first_lower = upper_rows * STRIDE
    upper_height = first_lower + STRIDE
    lower_height = lower_rows * STRIDE + STRIDE
    count, height = lax.axis_size("gz"), lax.axis_size("gy")
    peaks = jnp.transpose(peaks, (0, 2, 1, 3))[0]
    valid = jnp.transpose(valid, (1, 0, 2))

    constants = jnp.asarray(all_tables(columns // PATCH + 1, patch_columns), BF16)

    vmem = pl.BlockSpec(memory_space=pltpu.VMEM)

    def grant(mib):
        return pltpu.CompilerParams(vmem_limit_bytes=mib << 20)

    def shape(*dims, dtype=BF16):
        return jax.ShapeDtypeStruct(dims, dtype)

    merged = count == 2
    early, late, last = shape(upper_height, PATCH), shape(upper_height, columns - 2 * PATCH), shape(upper_height, PATCH)
    hbm = pl.BlockSpec(memory_space=pltpu.HBM)

    def held(value):
        return pltpu.with_memory_space_constraint(value, pltpu.HBM)

    copies = 3 + columns // PATCH + 5 + 3
    outs = pl.pallas_call(
        functools.partial(prepare_kernel, upper_rows, merged, count),
        out_shape=((early, late, last) if merged else (early, late, last, early, late))
        + (shape(STRIDE, columns), shape(rows, PATCH)),
        in_specs=[hbm] * 2,
        out_specs=(vmem,) * (5 if merged else 7),
        scratch_shapes=[
            pltpu.VMEM(peaks.shape, jnp.int32),
            pltpu.VMEM((SLOT, PATCH), F32),
            pltpu.SemaphoreType.DMA((copies,)),
        ],
        compiler_params=grant(1),
        name="prepare",
    )(held(tile), held(peaks))
    top, left = outs[-2:]

    up = [((s + 1) * height + y, s * height + y) for s in range(count - 1) for y in range(height)]
    down = [(s * height + y + 1, (s + 1) * height + y) for s in range(count - 1) for y in range(height - 1)]
    if merged:
        early_upper = early_lower = lax.ppermute(outs[0], ("gz", "gy"), up + down)
        late_upper = late_lower = lax.ppermute(outs[1], "gz", [(0, 1), (1, 0)])
    else:
        early_upper = lax.ppermute(outs[0], ("gz", "gy"), up)
        early_lower = lax.ppermute(outs[3], ("gz", "gy"), down)
        late_upper = passed_along(outs[1], "gz", -1)
        late_lower = passed_along(outs[4], "gz", 1)
    last_upper = passed_along(outs[2], "gz", -1)
    below = passed_along(top, "gy", -1)
    others = jnp.pad(early_upper[:, :STRIDE], ((0, rows + STRIDE - upper_height), (0, 0)))
    ours = jnp.concatenate([left[:, :STRIDE], below[:, :STRIDE]], 0)
    beside = passed_along(jnp.concatenate([ours, others], 1), "gx", -1)
    edge_lower = passed_along(side_by_side(beside[first_lower : rows + STRIDE]), "gz", 1)

    steps = patch_rows // 2
    depth = 2 * pairs * PATCH + 2 * SLOT
    width = columns + PATCH
    own_cost = pl.CostEstimate(flops=2_000_000_000, bytes_accessed=6_000_000, transcendentals=0)
    own_inner = pl.pallas_call(
        functools.partial(own_inner_kernel, upper_rows, count),
        out_shape=(shape(steps, depth, 2 * PATCH), shape(rows, columns), shape(*constants.shape)),
        in_specs=[hbm] * 2,
        out_specs=(vmem,) * 3,
        scratch_shapes=[pltpu.VMEM((2, depth, 2 * PATCH), BF16), pltpu.SemaphoreType.DMA((2,))],
        compiler_params=grant(6),
        cost_estimate=own_cost,
        name="own_inner",
    )
    spectra, tile, constants = own_inner(held(tile), held(constants))
    own_rest = pl.pallas_call(
        functools.partial(own_rest_kernel, upper_rows, count),
        out_shape=(shape(steps, depth, 2 * PATCH), shape(2, 8, PATCH, dtype=F32)),
        in_specs=[vmem] * 5,
        out_specs=(vmem, vmem),
        scratch_shapes=[
            pltpu.VMEM((rows + STRIDE, PATCH), BF16),
            pltpu.VMEM((8, width), F32),
            pltpu.VMEM((2, depth, 2 * PATCH), BF16),
        ],
        input_output_aliases={4: 0},
        compiler_params=grant(6),
        cost_estimate=own_cost,
        name="own_rest",
    )
    spectra, energy = own_rest(tile, below, beside, constants, spectra)

    def correlated(slot, chosen, first_row, count_rows, strip_rows, peaks_here, *pieces):
        size = count_rows * SLOT
        return pl.pallas_call(
            functools.partial(pair_kernel, slot, chosen, first_row, count_rows, patch_columns, count),
            out_shape=shape(8, PATCH, dtype=F32),
            in_specs=[pl.BlockSpec(memory_space=pl.ANY)] + [vmem] * 7,
            out_specs=vmem,
            scratch_shapes=[
                pltpu.SMEM((count_rows, 2, patch_columns), jnp.int32),
                pltpu.SemaphoreType.DMA,
                pltpu.VMEM((strip_rows, PATCH), BF16),
                pltpu.VMEM((8, width), F32),
                pltpu.VMEM((2, depth, 2 * PATCH), BF16),
                pltpu.VMEM((2, depth, 2 * PATCH), BF16),
                pltpu.VMEM((2, depth, 2 * PATCH), BF16),
                pltpu.VMEM((PATCH, PATCH), F32),
                pltpu.VMEM((size * 8, PATCH), F32),
                pltpu.VMEM((size, PATCH), jnp.int32),
            ]
            + [pltpu.VMEM((PATCH + 2 * EDGE, PATCH), F32)] * (4 * len(chosen)),
            compiler_params=grant(12),
            cost_estimate=pl.CostEstimate(flops=4_000_000_000, bytes_accessed=6_000_000, transcendentals=0),
        )(peaks_here, *pieces, spectra, energy, constants)

    at = lower_rows * STRIDE + 2 * (2 * lower_rows * STRIDE - upper_height)
    lanes = 2 * PATCH
    peaks_lower = late_lower[at : at + 2 * lower_rows, lanes : lanes + patch_columns].astype(jnp.int32)
    peaks_lower = peaks_lower.reshape(lower_rows, 2, patch_columns)
    lower = correlated(
        1, range(pairs), upper_rows, lower_rows, lower_height, peaks_lower, early_lower, late_lower,
        early_lower, edge_lower,
    )
    lower = passed_along(lower, "gz", -1)
    split = pairs - 2
    pieces = (early_upper, late_upper)
    upper_left = correlated(0, range(split), 0, upper_rows, upper_height, peaks, *pieces, early_upper, early_upper)
    upper_right = correlated(0, range(split, pairs), 0, upper_rows, upper_height, peaks, *pieces, last_upper, beside)
    fit = pl.pallas_call(
        functools.partial(join_kernel, upper_rows, 2 * split),
        out_shape=shape(6, patch_rows, 1, patch_columns, dtype=F32),
        in_specs=[vmem] * 4,
        out_specs=vmem,
        compiler_params=grant(1),
        name="join",
    )(upper_left, upper_right, lower, valid)
    return jnp.transpose(fit, (2, 0, 1, 3))


def solution(mesh):
    in_specs = (P("gz", "gy", "gx"), P("gz", None, "gy", "gx"), P("gz", "gy", "gx"))
    out_specs = P("gz", None, "gy", "gx")
    return jax.shard_map(body, mesh=mesh, in_specs=in_specs, out_specs=out_specs, check_vma=False)
```

```python
import functools
import math

import jax
import jax.numpy as jnp
import numpy as np
from jax import lax
from jax.experimental import pallas as pl
from jax.experimental.pallas import tpu as pltpu
from jax.sharding import PartitionSpec as P


PATCH = 128
STRIDE = 64
WIN = 5
HALF = PATCH // 2
EDGE = 8
SLOT = 16
PARTS = 2
F32 = jnp.float32
BF16 = jnp.bfloat16


def tables():
    index = np.arange(PATCH)
    phase = (index[:, None] * index[None, :] % PATCH).astype(np.float64) * (2.0 * math.pi / PATCH)
    cosine = np.asarray(np.cos(phase), dtype=jnp.bfloat16).astype(np.float32)
    sine = np.asarray(np.sin(phase), dtype=jnp.bfloat16).astype(np.float32)
    first = np.zeros((4 * HALF, 2 * PATCH), np.float32)
    for part, table in enumerate((cosine, -sine)):
        for which in range(2):
            top = part * PATCH + which * HALF
            first[top : top + HALF, which * STRIDE : which * STRIDE + PATCH] = table[:HALF]
    second = np.block([[cosine, -sine], [sine, cosine]])
    third = np.block([[cosine, sine], [-sine, cosine]])
    weight = np.where(np.arange(HALF) == 0, 1.0, 2.0)[None, :]
    fourth = np.concatenate(
        [cosine[:, :HALF] * weight, -sine[:, :HALF] * weight, np.repeat(cosine[:, HALF : HALF + 1], SLOT, 1)], 1
    )
    return first, second, third, fourth, cosine[HALF]


def middle_rows(middle, pairs):
    rows = np.zeros((pairs, SLOT, 2 * PATCH), np.float32)
    for pair in range(pairs):
        for which in range(2):
            rows[pair, 2 * pair + which, which * STRIDE : which * STRIDE + PATCH] = middle
    return rows


def columns_mask(blocks, columns):
    mask = np.zeros((blocks * PATCH, PATCH), np.float32)
    for column in range(columns):
        mask[column * STRIDE : column * STRIDE + PATCH, column] = 1.0
    return mask


class Tables:
    def __init__(self, ref, pairs):
        self.ref, self.pairs = ref, pairs

    def rows(self, top, count):
        return self.ref[top : top + count, :]

    def first(self):
        return self.rows(0, 2 * PATCH)

    def middle(self, pair):
        return self.rows(6 * PATCH + PATCH + pair * SLOT, SLOT)

    def second(self):
        return self.rows(2 * PATCH, 2 * PATCH)

    def third(self):
        return self.rows(4 * PATCH, 2 * PATCH)

    def fourth(self):
        return self.ref[6 * PATCH : 7 * PATCH, : PATCH + SLOT]

    def mask(self):
        value = self.rows(7 * PATCH + self.pairs * SLOT, (self.pairs + 1) * PATCH // 2)
        return jnp.concatenate([value[:, :PATCH], value[:, PATCH:]], 0)


def all_tables(blocks, columns):
    first, second, third, fourth, middle = tables()
    fourth = np.pad(fourth, ((0, 0), (0, 2 * PATCH - fourth.shape[1])))
    mask = columns_mask(blocks, columns)
    half = mask.shape[0] // 2
    return np.concatenate(
        [
            first, second, third, fourth, middle_rows(middle, columns // 2).reshape(-1, 2 * PATCH),
            np.concatenate([mask[:half], mask[half:]], 1),
        ],
        0,
    )


def passed_along(value, axis, steps):
    count = lax.axis_size(axis)
    initial, last = (max(0, -steps), min(count, count - steps))
    return lax.ppermute(value, axis, [(source, source + steps) for source in range(initial, last)])


def two_terms(value):
    high = value.astype(BF16)
    return high, (value - high.astype(F32)).astype(BF16)


def only_low(value):
    low = lax.broadcasted_iota(jnp.int32, value.shape, 1) < STRIDE
    return jnp.where(low, value.astype(F32), 0.0).astype(BF16)


def working(count):
    position = lax.axis_index("gz")
    return position < count - 1, position > 0


def start_all(copies):
    for copy in copies:
        copy.start()


def wait_all(copies):
    for copy in copies:
        copy.wait()


def parts(rows, first=0):
    step = (rows - first) // PARTS
    return [slice(top, top + step) for top in range(first, rows, step)]


def window_of(chunk, start, block):
    return jnp.concatenate([chunk(start, block), chunk(start + 1, block)], 0)


def forward(chunk, start, table, columns_of, chosen=None):
    pairs = table.pairs
    total = jnp.zeros((SLOT, 2 * PATCH), F32)
    for pair in range(pairs) if chosen is None else chosen:
        right = jnp.concatenate(
            [
                jnp.concatenate([window_of(chunk, start + w, pair + half) for half in range(2)], 1)
                for w in range(2)
            ],
            0,
        )
        left = jnp.concatenate([table.first(), table.middle(pair)], 0)
        out = lax.dot_general(left, right, (((1,), (1,)), ((), ())), preferred_element_type=F32)
        one = out[: 2 * PATCH].astype(BF16)
        for w in range(2):
            top = (2 * pair + w) * PATCH
            columns_of[top : top + PATCH, :PATCH] = one[:PATCH, w * PATCH : (w + 1) * PATCH]
            columns_of[top : top + PATCH, PATCH:] = one[PATCH:, w * PATCH : (w + 1) * PATCH]
        total += out[2 * PATCH :]
    value = total.astype(BF16)
    top = 2 * pairs * PATCH
    for w in range(2):
        columns_of[top + w * SLOT : top + (w + 1) * SLOT, :PATCH] = value[:, w * PATCH : (w + 1) * PATCH]
    columns_of[top : top + 2 * SLOT, PATCH:] = jnp.zeros((2 * SLOT, PATCH), BF16)


def energies(chunk, blocks, first_row, patch_rows, mask, sums):
    for row in range(patch_rows + 1):
        for block in blocks:
            pixels = chunk(first_row + row, block).astype(F32)
            sums[row : row + 1, block * PATCH : (block + 1) * PATCH] = jnp.sum(pixels * pixels, axis=0, keepdims=True)
    lanes = slice(blocks[0] * PATCH, (blocks[-1] + 1) * PATCH)
    both = sums[0:patch_rows, lanes] + sums[1 : patch_rows + 1, lanes]
    total = sum(jnp.dot(term, mask[lanes], preferred_element_type=F32) for term in two_terms(both))
    return total * (1.0 / (PATCH * PATCH))


def prepare_kernel(upper_rows, merged, count, tile, peaks, *refs):
    rows, columns = tile.shape
    patch_rows = rows // STRIDE
    height = (upper_rows + 1) * STRIDE
    first_lower = upper_rows * STRIDE
    lower = rows - first_lower
    sends = 3 if merged else 5
    outs, (side, top, left), (numbers, packed, sems) = refs[:sends], refs[sends : sends + 3], refs[sends + 3 :]
    up, down = outs[:3], outs[:2] if merged else outs[3:]
    blocks = columns // PATCH
    inside = blocks - 2
    _, has_before = working(count)

    def lanes(block):
        return slice(block * PATCH, (block + 1) * PATCH)

    upwards = [
        (tile.at[:height, lanes(0)], up[0]),
        (tile.at[:height, PATCH : PATCH * (blocks - 1)], up[1]),
        (tile.at[:height, lanes(blocks - 1)], up[2]),
    ]
    early, late = down
    tall = height - lower
    downwards = [(tile.at[:STRIDE, lanes(b)], early.at[b * STRIDE : (b + 1) * STRIDE, :]) for b in range(blocks)]
    downwards.append((tile.at[first_lower:, : inside * PATCH], late.at[:lower, :]))
    for k in range(2):
        source = lanes(inside + k)
        downwards.append((tile.at[first_lower : first_lower + tall, source], late.at[lower:, lanes(k)]))
        at = lower + k * (lower - tall)
        downwards.append((tile.at[first_lower + tall :, source], late.at[at : at + lower - tall, lanes(2)]))
    peaks_at = lower + 2 * (lower - tall)

    def add_peaks():
        packed[...] = jnp.zeros_like(packed)
        for i in range(patch_rows - upper_rows):
            packed[2 * i : 2 * i + 2, : peaks.shape[2]] = numbers[upper_rows + i].astype(F32)
        late[peaks_at : peaks_at + SLOT, lanes(2)] = packed[...].astype(BF16)

    fixed = [
        (peaks, numbers),
        (tile.at[first_lower:, :PATCH], side),
        (tile.at[:STRIDE, :], top),
        (tile.at[:, :PATCH], left),
    ]
    groups = []
    used = 0
    for group in (upwards, downwards, fixed):
        groups.append([pltpu.make_async_copy(a, b, sems.at[used + k]) for k, (a, b) in enumerate(group)])
        used += len(group)
    upwards, downwards, fixed = groups
    if merged:
        pl.when(has_before)(lambda: start_all(upwards))
        pl.when(jnp.logical_not(has_before))(lambda: start_all(downwards))
        start_all(fixed)
        fixed[0].wait()
        pl.when(jnp.logical_not(has_before))(add_peaks)
        pl.when(has_before)(lambda: wait_all(upwards))
        pl.when(jnp.logical_not(has_before))(lambda: wait_all(downwards))
        wait_all(fixed[1:])
    else:
        start_all(fixed + upwards + downwards)
        fixed[0].wait()
        add_peaks()
        wait_all(fixed[1:] + upwards + downwards)


def own_inner_kernel(
    upper_rows, left_pairs, count, source, tables_source, spectra, tile, constants, energy, sums, once, sems
):
    rows, columns = tile.shape
    patch_rows = rows // STRIDE
    blocks = columns // PATCH
    table = Tables(constants, blocks)

    def chunk(row, block):
        return tile[row * STRIDE : (row + 1) * STRIDE, block * PATCH : (block + 1) * PATCH]

    copies = [
        pltpu.make_async_copy(source, tile, sems.at[0]),
        pltpu.make_async_copy(tables_source, constants, sems.at[1]),
    ]
    start_all(copies)
    wait_all(copies)
    active = working(count)
    inner = 2 * (blocks - 1) * PATCH
    for slot, (lowest, highest) in enumerate(((0, upper_rows), (upper_rows, patch_rows - 2))):

        @pl.when(active[slot])
        def _(slot=slot, lowest=lowest, highest=highest):
            for step in range(lowest // 2, highest // 2):
                columns_of = once.at[step % 2]
                forward(chunk, 2 * step, table, columns_of, range(blocks - 1))
                depth = columns_of.shape[0]
                for part in parts(inner) + [slice(depth - 2 * SLOT, depth)]:
                    value = jnp.dot(columns_of[part, :], table.second(), preferred_element_type=F32)
                    spectra[step, part, :] = value.astype(BF16)
            if slot == 0:
                energy[0, :upper_rows, :] = energies(
                    chunk, range(left_pairs + 1), 0, upper_rows, table.mask(), sums
                )


def own_below_kernel(
    upper_rows, left_pairs, count, tile, below, constants, started, early_energy, spectra, energy, sums, once
):
    rows, columns = tile.shape
    patch_rows = rows // STRIDE
    blocks = columns // PATCH
    table = Tables(constants, blocks)

    def chunk(row, block):
        lanes = slice(block * PATCH, (block + 1) * PATCH)
        return tile[row * STRIDE : (row + 1) * STRIDE, lanes] if row < patch_rows else below[:, lanes]

    inner = 2 * (blocks - 1) * PATCH
    step = patch_rows // 2 - 1

    @pl.when(working(count)[1])
    def _():
        columns_of = once
        forward(chunk, 2 * step, table, columns_of, range(blocks - 1))
        depth = columns_of.shape[0]
        for part in parts(inner) + [slice(depth - 2 * SLOT, depth)]:
            value = jnp.dot(columns_of[part, :], table.second(), preferred_element_type=F32)
            spectra[step, part, :] = value.astype(BF16)
        energy[1, : patch_rows - upper_rows, :] = energies(
            chunk, range(left_pairs + 1), upper_rows, patch_rows - upper_rows, table.mask(), sums
        )


def own_rest_kernel(
    upper_rows, left_pairs, count, tile, below, beside, constants, started, after_upper, after_lower, spectra, energy,
    strip, sums, once
):
    rows, columns = tile.shape
    patch_rows = rows // STRIDE
    blocks = columns // PATCH
    table = Tables(constants, blocks)
    strip[...] = only_low(beside[...])
    active = working(count)

    def chunk(row, block):
        at = slice(row * STRIDE, (row + 1) * STRIDE)
        if block == blocks:
            return strip[at, :]
        lanes = slice(block * PATCH, (block + 1) * PATCH)
        return tile[at, lanes] if row < patch_rows else below[:, lanes]

    inner = 2 * (blocks - 1) * PATCH
    for slot, (lowest, highest) in enumerate(((0, upper_rows), (upper_rows, patch_rows))):

        @pl.when(active[slot])
        def _(slot=slot, lowest=lowest, highest=highest):
            for step in range(lowest // 2, highest // 2):
                columns_of = once.at[step % 2]
                depth = columns_of.shape[0]
                forward(chunk, 2 * step, table, columns_of, [blocks - 1])
                for part in parts(depth, inner):
                    value = jnp.dot(columns_of[part, :], table.second(), preferred_element_type=F32)
                    middle = max(part.start, depth - 2 * SLOT)
                    if part.stop <= middle:
                        spectra[step, part, :] = value.astype(BF16)
                    else:
                        size = part.stop - middle
                        spectra[step, part.start : middle, :] = value[:-size].astype(BF16)
                        before = spectra[step, middle : part.stop, :].astype(F32)
                        spectra[step, middle : part.stop, :] = (before + value[-size:]).astype(BF16)
            energy[slot, : highest - lowest, :] = energies(
                chunk, range(left_pairs, blocks + 1), lowest, highest - lowest, table.mask(), sums
            )


def crossed(own, other, flipped):
    own = own.astype(F32)
    own_re, own_im = own[:, :PATCH], own[:, PATCH:]
    re, im = other[:, :PATCH], other[:, PATCH:]
    real = own_re * re + own_im * im
    imaginary = own_im * re - own_re * im if flipped else own_re * im - own_im * re
    return jnp.concatenate([real.astype(BF16), imaginary.astype(BF16)], 1)


def pair_kernel(
    slot, chosen, first_row, patch_rows, patch_columns, count, corner, peaks_source, early, late, last, beside, left, spectra,
    energy, constants, out, peaks, sem, strip, sums, once, crosses, inverse, peak, moments, offsets, *surfaces
):
    flipped = slot == 1
    size = patch_rows * SLOT
    pairs = patch_columns // 2
    blocks = pairs
    table = Tables(constants, pairs)
    active = working(count)[slot]
    patches = range(2 * chosen[0], 2 * chosen[-1] + 2)

    @pl.when(jnp.logical_not(active))
    def _():
        out[...] = jnp.zeros_like(out)

    @pl.when(active)
    def _():
        fetch = pltpu.make_async_copy(peaks_source.at[:patch_rows], peaks, sem)
        fetch.start()
        if chosen[-1] == pairs - 1:
            if flipped:
                most = patch_rows * STRIDE
                strip[:most, :] = only_low(last[...])
                packed = beside[corner : corner + STRIDE, :].astype(F32)
                strip[most:, :] = only_low(pltpu.roll(packed, STRIDE, 1))
            else:
                packed = beside[: strip.shape[0], :].astype(F32)
                strip[...] = only_low(pltpu.roll(packed, STRIDE, 1))

        def lanes_of(block):
            return slice(block * PATCH, (block + 1) * PATCH)

        def chunk(row, block):
            at = slice(row * STRIDE, (row + 1) * STRIDE)
            if block == blocks:
                return strip[at, :]
            if not flipped:
                if block == 0:
                    return early[at, :]
                return last[at, :] if block == blocks - 1 else late[at, lanes_of(block - 1)]
            if row == patch_rows:
                return early[block * STRIDE : (block + 1) * STRIDE, :]
            inside = blocks - 2
            if block < inside:
                return late[at, lanes_of(block)]
            lower = patch_rows * STRIDE
            tall = late.shape[0] - lower
            start = row * STRIDE
            if start < tall:
                return late[lower + start : lower + start + STRIDE, lanes_of(block - inside)]
            start += lower + (block - inside) * (lower - tall) - tall
            return late[start : start + STRIDE, lanes_of(2)]

        row_of = lax.broadcasted_iota(jnp.int32, (SLOT, 2 * PATCH), 0)
        for step in range(patch_rows // 2):
            columns_of, cross, back = once.at[step % 2], crosses.at[step % 2], inverse.at[step % 2]
            forward(chunk, 2 * step, table, columns_of, chosen)
            depth = columns_of.shape[0]
            if len(chosen) == pairs:
                rows = parts(depth)
            else:
                rows = parts(patches.stop * PATCH, patches.start * PATCH) + [slice(depth - 2 * SLOT, depth)]
            for part in rows:
                spectrum = jnp.dot(columns_of[part, :], table.second(), preferred_element_type=F32)
                cross[part, :] = crossed(spectra[step + first_row // 2, part, :], spectrum, flipped)
            for part in rows:
                back[part, :] = jnp.dot(cross[part, :], table.third(), preferred_element_type=F32).astype(BF16)
            top = 2 * pairs * PATCH
            mid = back[top : top + 2 * SLOT, :PATCH].astype(F32)
            mid = jnp.concatenate([mid[:SLOT], mid[SLOT:]], 1)
            if step == 0:
                fetch.wait()
            for column in patches:
                a = (column // 2) * 2 * PATCH + (column % 2) * HALF
                b = a + PATCH
                right = jnp.concatenate(
                    [
                        jnp.concatenate([back[a : a + HALF, :PATCH], back[b : b + HALF, :PATCH]], 1),
                        jnp.concatenate([back[a : a + HALF, PATCH:], back[b : b + HALF, PATCH:]], 1),
                        jnp.where(row_of == column, mid, 0.0).astype(BF16),
                    ],
                    0,
                )
                value = jnp.dot(table.fourth(), right, preferred_element_type=F32)
                largest = jnp.max(jnp.abs(value), axis=0, keepdims=True)
                for which in range(2):
                    lanes = slice(which * PATCH, (which + 1) * PATCH)
                    i = 2 * step + which
                    at = i * SLOT + column
                    surface = surfaces[2 * (column - patches.start) + which]
                    surface[EDGE : EDGE + PATCH, :] = value[:, lanes]
                    surface[:EDGE, :] = value[PATCH - EDGE :, lanes]
                    surface[EDGE + PATCH :, :] = value[:EDGE, lanes]
                    peak[at : at + 1, :] = largest[:, lanes]
                    along = peaks[i, 1, column] + (EDGE - WIN // 2)
                    moments[at * 8 : at * 8 + 8, :] = surface[pl.ds(along, 8), :]
                    offsets[at : at + 1, :] = jnp.full((1, PATCH), peaks[i, 0, column], jnp.int32)
        other = energies(chunk, range(chosen[0], chosen[-1] + 2), 0, patch_rows, table.mask(), sums)
        scales = float(PATCH) ** 3 * jnp.sqrt((energy[slot, :patch_rows, :] + 1e-05) * (other + 1e-05))

        lane = lax.broadcasted_iota(jnp.int32, (1, PATCH), 1)
        scale = jnp.ones((1, PATCH), F32)
        for i in range(patch_rows):
            row = scales[i : i + 1, :]
            row = pltpu.roll(row, i * SLOT, 1) if i else row
            scale = jnp.where((lane >= i * SLOT + patches.start) & (lane < i * SLOT + patches.stop), row, scale)
        peak_rows = peak[...]
        height = jnp.max(jnp.transpose(peak_rows), axis=0, keepdims=True) / scale + 1e-05

        lane = lax.broadcasted_iota(jnp.int32, (size, PATCH), 1)
        offset = (lane - offsets[...] + (WIN // 2 + PATCH)) & (PATCH - 1)
        u = (offset - WIN // 2).astype(F32)
        within = offset < WIN
        numbers = np.arange(WIN) - WIN // 2
        middle_square = float(np.mean(numbers**2))
        u0 = jnp.where(within, 1.0, 0.0)
        u1 = jnp.where(within, u, 0.0)
        u2 = jnp.where(within, u * u - middle_square, 0.0)
        v0 = v1 = v2 = jnp.zeros((size, PATCH), F32)
        for v in range(WIN):
            value = moments[pl.ds(v, size, stride=8), :]
            position = float(v - WIN // 2)
            v0 += value
            v1 += position * value
            v2 += (position * position - middle_square) * value
        factors = ((u0, v0), (u1, v0), (u0, v1), (u2, v0), (u0, v2), (u1, v1))
        terms = [two_terms(fu * fv) for fu, fv in factors]
        which_e = lax.broadcasted_iota(jnp.int32, (SLOT, len(terms) * PATCH), 0)
        of_lane = lax.broadcasted_iota(jnp.int32, (SLOT, len(terms) * PATCH), 1)
        ones = jnp.where((of_lane >= which_e * PATCH) & (of_lane < (which_e + 1) * PATCH), 1.0, 0.0).astype(BF16)
        total = sum(
            lax.dot_general(
                ones, jnp.concatenate([t[k] for t in terms], 1), (((1,), (1,)), ((), ())), preferred_element_type=F32
            )
            for k in range(2)
        )[:8]
        linear = float(np.sum(numbers**2))
        quadratic = float(np.sum((numbers**2 - middle_square) ** 2))
        norms = (
            float(WIN), math.sqrt(WIN * linear), math.sqrt(WIN * linear), math.sqrt(WIN * quadratic),
            math.sqrt(WIN * quadratic), linear,
        )
        e_row = lax.broadcasted_iota(jnp.int32, (8, size), 0)
        factor = jnp.zeros((8, size), F32)
        for e, norm in enumerate(norms):
            factor = jnp.where(e_row == e, 1.0 / norm, factor)
        result = total * factor / (scale * height)[:, :size]
        if chosen[0] > 0:
            slot_lane = lax.broadcasted_iota(jnp.int32, (8, size), 1) & (SLOT - 1)
            result = jnp.where(slot_lane < patches.start, left[:, :size], result)
        out[:, :size] = result
        if size < PATCH:
            out[:, size:] = jnp.zeros((8, PATCH - size), F32)


def join_kernel(upper_rows, upper, lower, valid, out):
    count, patch_rows, _, patch_columns = out.shape
    for i in range(patch_rows):
        source, at = (upper, i) if i < upper_rows else (lower, i - upper_rows)
        value = source[...]
        turned = pltpu.roll(value, PATCH - at * SLOT, 1) if at else value
        keep = valid[i].astype(F32)
        for e in range(count):
            out[e, i] = turned[e : e + 1, :patch_columns] * keep


def body(sections, peaks, valid):
    tile = sections[0]
    rows, columns = tile.shape
    patch_rows, patch_columns = rows // STRIDE, columns // STRIDE
    pairs = patch_columns // 2
    upper_rows = (patch_rows // 2 + 1) // 2 * 2
    lower_rows = patch_rows - upper_rows
    first_lower = upper_rows * STRIDE
    upper_height = first_lower + STRIDE
    lower_height = lower_rows * STRIDE + STRIDE
    count, height = lax.axis_size("gz"), lax.axis_size("gy")
    peaks = jnp.transpose(peaks, (0, 2, 1, 3))[0]
    valid = jnp.transpose(valid, (1, 0, 2))

    constants = jnp.asarray(all_tables(columns // PATCH + 1, patch_columns), BF16)

    vmem = pl.BlockSpec(memory_space=pltpu.VMEM)

    def grant(mib):
        return pltpu.CompilerParams(vmem_limit_bytes=mib << 20)

    def shape(*dims, dtype=BF16):
        return jax.ShapeDtypeStruct(dims, dtype)

    merged = count == 2
    early, late, last = shape(upper_height, PATCH), shape(upper_height, columns - 2 * PATCH), shape(upper_height, PATCH)
    hbm = pl.BlockSpec(memory_space=pltpu.HBM)

    def held(value):
        return pltpu.with_memory_space_constraint(value, pltpu.HBM)

    copies = 3 + columns // PATCH + 5 + 4
    outs = pl.pallas_call(
        functools.partial(prepare_kernel, upper_rows, merged, count),
        out_shape=((early, late, last) if merged else (early, late, last, early, late))
        + (shape(rows - first_lower, PATCH), shape(STRIDE, columns), shape(rows, PATCH)),
        in_specs=[hbm] * 2,
        out_specs=(vmem,) * (6 if merged else 8),
        scratch_shapes=[
            pltpu.VMEM(peaks.shape, jnp.int32),
            pltpu.VMEM((SLOT, PATCH), F32),
            pltpu.SemaphoreType.DMA((copies,)),
        ],
        compiler_params=grant(1),
        name="prepare",
    )(held(tile), held(peaks))
    side, top, left = outs[-3:]

    up = [((s + 1) * height + y, s * height + y) for s in range(count - 1) for y in range(height)]
    down = [(s * height + y + 1, (s + 1) * height + y) for s in range(count - 1) for y in range(height - 1)]
    across = lax.axis_size("gx")
    slant = [(s * across + x + 1, (s + 1) * across + x) for s in range(count - 1) for x in range(across - 1)]
    side = lax.ppermute(side, ("gz", "gx"), slant)
    if merged:
        early_upper = early_lower = lax.ppermute(outs[0], ("gz", "gy"), up + down)
        late_upper = late_lower = lax.ppermute(outs[1], "gz", [(0, 1), (1, 0)])
    else:
        early_upper = lax.ppermute(outs[0], ("gz", "gy"), up)
        early_lower = lax.ppermute(outs[3], ("gz", "gy"), down)
        late_upper = passed_along(outs[1], "gz", -1)
        late_lower = passed_along(outs[4], "gz", 1)
    last_upper = passed_along(outs[2], "gz", -1)
    steps_up = [(s * height + y + 1, s * height + y) for s in range(1, count) for y in range(height - 1)]
    below = lax.ppermute(top, ("gz", "gy"), steps_up)
    others = jnp.concatenate([early_upper[:, :STRIDE], early_lower[:STRIDE, :STRIDE]], 0)
    others = jnp.pad(others, ((0, rows - upper_height), (0, 0)))
    ours = jnp.concatenate([left[:, :STRIDE], below[:, :STRIDE]], 0)
    beside = passed_along(jnp.concatenate([ours, others], 1), "gx", -1)
    steps = patch_rows // 2
    depth = 2 * pairs * PATCH + 2 * SLOT
    width = columns + PATCH
    split = pairs - 2
    own_cost = pl.CostEstimate(flops=2_000_000_000, bytes_accessed=6_000_000, transcendentals=0)
    own_inner = pl.pallas_call(
        functools.partial(own_inner_kernel, upper_rows, split, count),
        out_shape=(
            shape(steps, depth, 2 * PATCH), shape(rows, columns), shape(*constants.shape), shape(2, 8, PATCH, dtype=F32)
        ),
        in_specs=[hbm] * 2,
        out_specs=(vmem,) * 4,
        scratch_shapes=[pltpu.VMEM((8, width), F32), pltpu.VMEM((2, depth, 2 * PATCH), BF16), pltpu.SemaphoreType.DMA((2,))],
        compiler_params=grant(6),
        cost_estimate=own_cost,
        name="own_inner",
    )
    spectra, tile, constants, energy_left = own_inner(held(tile), held(constants))

    def correlated(slot, chosen, first_row, count_rows, strip_rows, peaks_here, spectra, energy, *pieces):
        size = count_rows * SLOT
        return pl.pallas_call(
            functools.partial(pair_kernel, slot, chosen, first_row, count_rows, patch_columns, count, upper_height),
            out_shape=shape(8, PATCH, dtype=F32),
            in_specs=[pl.BlockSpec(memory_space=pl.ANY)] + [vmem] * 8,
            out_specs=vmem,
            scratch_shapes=[
                pltpu.SMEM((count_rows, 2, patch_columns), jnp.int32),
                pltpu.SemaphoreType.DMA,
                pltpu.VMEM((strip_rows, PATCH), BF16),
                pltpu.VMEM((8, width), F32),
                pltpu.VMEM((2, depth, 2 * PATCH), BF16),
                pltpu.VMEM((2, depth, 2 * PATCH), BF16),
                pltpu.VMEM((2, depth, 2 * PATCH), BF16),
                pltpu.VMEM((PATCH, PATCH), F32),
                pltpu.VMEM((size * 8, PATCH), F32),
                pltpu.VMEM((size, PATCH), jnp.int32),
            ]
            + [pltpu.VMEM((PATCH + 2 * EDGE, PATCH), F32)] * (4 * len(chosen)),
            compiler_params=grant(12),
            cost_estimate=pl.CostEstimate(flops=4_000_000_000, bytes_accessed=6_000_000, transcendentals=0),
        )(peaks_here, *pieces, spectra, energy, constants)

    own_below = pl.pallas_call(
        functools.partial(own_below_kernel, upper_rows, split, count),
        out_shape=(shape(steps, depth, 2 * PATCH), shape(2, 8, PATCH, dtype=F32)),
        in_specs=[vmem] * 5,
        out_specs=(vmem, vmem),
        scratch_shapes=[pltpu.VMEM((8, width), F32), pltpu.VMEM((depth, 2 * PATCH), BF16)],
        input_output_aliases={3: 0, 4: 1},
        compiler_params=grant(4),
        cost_estimate=own_cost,
        name="own_below",
    )
    spectra, energy_left = own_below(tile, below, constants, spectra, energy_left)
    at = lower_rows * STRIDE + 2 * (2 * lower_rows * STRIDE - upper_height)
    lanes = 2 * PATCH
    peaks_lower = late_lower[at : at + 2 * lower_rows, lanes : lanes + patch_columns].astype(jnp.int32)
    peaks_lower = peaks_lower.reshape(lower_rows, 2, patch_columns)
    upper_part = (0, upper_rows, upper_height, peaks)
    lower_part = (upper_rows, lower_rows, lower_height, peaks_lower)
    nothing = energy_left[0]
    upper_left = correlated(
        0, range(split), *upper_part, spectra, energy_left, early_upper, late_upper, nothing, nothing, nothing
    )
    lower_left = correlated(
        1, range(split), *lower_part, spectra, energy_left, early_lower, late_lower, nothing, nothing, nothing
    )
    own_rest = pl.pallas_call(
        functools.partial(own_rest_kernel, upper_rows, split, count),
        out_shape=(shape(steps, depth, 2 * PATCH), shape(2, 8, PATCH, dtype=F32)),
        in_specs=[vmem] * 7,
        out_specs=(vmem, vmem),
        scratch_shapes=[
            pltpu.VMEM((rows + STRIDE, PATCH), BF16),
            pltpu.VMEM((8, width), F32),
            pltpu.VMEM((2, depth, 2 * PATCH), BF16),
        ],
        input_output_aliases={4: 0},
        compiler_params=grant(6),
        cost_estimate=own_cost,
        name="own_rest",
    )
    spectra, energy = own_rest(tile, below, beside, constants, spectra, upper_left, lower_left)

    rest = range(split, pairs)
    lower = correlated(1, rest, *lower_part, spectra, energy, early_lower, late_lower, side, beside, lower_left)
    lower = passed_along(lower, "gz", -1)
    upper = correlated(0, rest, *upper_part, spectra, energy, early_upper, late_upper, last_upper, beside, upper_left)
    fit = pl.pallas_call(
        functools.partial(join_kernel, upper_rows),
        out_shape=shape(6, patch_rows, 1, patch_columns, dtype=F32),
        in_specs=[vmem] * 3,
        out_specs=vmem,
        compiler_params=grant(1),
        name="join",
    )(upper, lower, valid)
    return jnp.transpose(fit, (2, 0, 1, 3))


def solution(mesh):
    in_specs = (P("gz", "gy", "gx"), P("gz", None, "gy", "gx"), P("gz", "gy", "gx"))
    out_specs = P("gz", None, "gy", "gx")
    return jax.shard_map(body, mesh=mesh, in_specs=in_specs, out_specs=out_specs, check_vma=False)
```

```python
import functools
import math

import jax
import jax.numpy as jnp
import numpy as np
from jax import lax
from jax.experimental import pallas as pl
from jax.experimental.pallas import tpu as pltpu
from jax.sharding import PartitionSpec as P


PATCH = 128
STRIDE = 64
WIN = 5
HALF = PATCH // 2
EDGE = 8
SLOT = 16
PARTS = 2
F32 = jnp.float32
BF16 = jnp.bfloat16


def tables():
    index = np.arange(PATCH)
    phase = (index[:, None] * index[None, :] % PATCH).astype(np.float64) * (2.0 * math.pi / PATCH)
    cosine = np.asarray(np.cos(phase), dtype=jnp.bfloat16).astype(np.float32)
    sine = np.asarray(np.sin(phase), dtype=jnp.bfloat16).astype(np.float32)
    first = np.zeros((4 * HALF, 2 * PATCH), np.float32)
    for part, table in enumerate((cosine, -sine)):
        for which in range(2):
            top = part * PATCH + which * HALF
            first[top : top + HALF, which * STRIDE : which * STRIDE + PATCH] = table[:HALF]
    second = np.block([[cosine, -sine], [sine, cosine]])
    third = np.block([[cosine, sine], [-sine, cosine]])
    weight = np.where(np.arange(HALF) == 0, 1.0, 2.0)[None, :]
    fourth = np.concatenate(
        [cosine[:, :HALF] * weight, -sine[:, :HALF] * weight, np.repeat(cosine[:, HALF : HALF + 1], SLOT, 1)], 1
    )
    return first, second, third, fourth, cosine[HALF]


def middle_rows(middle, pairs):
    rows = np.zeros((pairs, SLOT, 2 * PATCH), np.float32)
    for pair in range(pairs):
        for which in range(2):
            rows[pair, 2 * pair + which, which * STRIDE : which * STRIDE + PATCH] = middle
    return rows


def columns_mask(blocks, columns):
    mask = np.zeros((blocks * PATCH, PATCH), np.float32)
    for column in range(columns):
        mask[column * STRIDE : column * STRIDE + PATCH, column] = 1.0
    return mask


class Tables:
    def __init__(self, ref, pairs):
        self.ref, self.pairs = ref, pairs

    def rows(self, top, count):
        return self.ref[top : top + count, :]

    def first(self):
        return self.rows(0, 2 * PATCH)

    def middle(self, pair):
        return self.rows(6 * PATCH + PATCH + pair * SLOT, SLOT)

    def second(self):
        return self.rows(2 * PATCH, 2 * PATCH)

    def third(self):
        return self.rows(4 * PATCH, 2 * PATCH)

    def fourth(self):
        return self.ref[6 * PATCH : 7 * PATCH, : PATCH + SLOT]

    def mask(self):
        value = self.rows(7 * PATCH + self.pairs * SLOT, (self.pairs + 1) * PATCH // 2)
        return jnp.concatenate([value[:, :PATCH], value[:, PATCH:]], 0)


def all_tables(blocks, columns):
    first, second, third, fourth, middle = tables()
    fourth = np.pad(fourth, ((0, 0), (0, 2 * PATCH - fourth.shape[1])))
    mask = columns_mask(blocks, columns)
    half = mask.shape[0] // 2
    return np.concatenate(
        [
            first, second, third, fourth, middle_rows(middle, columns // 2).reshape(-1, 2 * PATCH),
            np.concatenate([mask[:half], mask[half:]], 1),
        ],
        0,
    )


def passed_along(value, axis, steps):
    count = lax.axis_size(axis)
    initial, last = (max(0, -steps), min(count, count - steps))
    return lax.ppermute(value, axis, [(source, source + steps) for source in range(initial, last)])


def two_terms(value):
    high = value.astype(BF16)
    return high, (value - high.astype(F32)).astype(BF16)


def only_low(value):
    low = lax.broadcasted_iota(jnp.int32, value.shape, 1) < STRIDE
    return jnp.where(low, value.astype(F32), 0.0).astype(BF16)


def working(count):
    position = lax.axis_index("gz")
    return position < count - 1, position > 0


def start_all(copies):
    for copy in copies:
        copy.start()


def wait_all(copies):
    for copy in copies:
        copy.wait()


def parts(rows, first=0):
    step = (rows - first) // PARTS
    return [slice(top, top + step) for top in range(first, rows, step)]


def window_of(chunk, start, block):
    return jnp.concatenate([chunk(start, block), chunk(start + 1, block)], 0)


def forward(chunk, start, table, columns_of, chosen=None):
    pairs = table.pairs
    total = jnp.zeros((SLOT, 2 * PATCH), F32)
    for pair in range(pairs) if chosen is None else chosen:
        right = jnp.concatenate(
            [
                jnp.concatenate([window_of(chunk, start + w, pair + half) for half in range(2)], 1)
                for w in range(2)
            ],
            0,
        )
        left = jnp.concatenate([table.first(), table.middle(pair)], 0)
        out = lax.dot_general(left, right, (((1,), (1,)), ((), ())), preferred_element_type=F32)
        one = out[: 2 * PATCH].astype(BF16)
        for w in range(2):
            top = (2 * pair + w) * PATCH
            columns_of[top : top + PATCH, :PATCH] = one[:PATCH, w * PATCH : (w + 1) * PATCH]
            columns_of[top : top + PATCH, PATCH:] = one[PATCH:, w * PATCH : (w + 1) * PATCH]
        total += out[2 * PATCH :]
    value = total.astype(BF16)
    top = 2 * pairs * PATCH
    for w in range(2):
        columns_of[top + w * SLOT : top + (w + 1) * SLOT, :PATCH] = value[:, w * PATCH : (w + 1) * PATCH]
    columns_of[top : top + 2 * SLOT, PATCH:] = jnp.zeros((2 * SLOT, PATCH), BF16)


def energies(chunk, blocks, first_row, patch_rows, mask, sums):
    for row in range(patch_rows + 1):
        for block in blocks:
            pixels = chunk(first_row + row, block).astype(F32)
            sums[row : row + 1, block * PATCH : (block + 1) * PATCH] = jnp.sum(pixels * pixels, axis=0, keepdims=True)
    lanes = slice(blocks[0] * PATCH, (blocks[-1] + 1) * PATCH)
    both = sums[0:patch_rows, lanes] + sums[1 : patch_rows + 1, lanes]
    total = sum(jnp.dot(term, mask[lanes], preferred_element_type=F32) for term in two_terms(both))
    return total * (1.0 / (PATCH * PATCH))


def prepare_kernel(upper_rows, merged, count, tile, peaks, *refs):
    rows, columns = tile.shape
    patch_rows = rows // STRIDE
    height = (upper_rows + 1) * STRIDE
    first_lower = upper_rows * STRIDE
    lower = rows - first_lower
    sends = 3 if merged else 5
    outs, (side, top, left), (numbers, packed, sems) = refs[:sends], refs[sends : sends + 3], refs[sends + 3 :]
    up, down = outs[:3], outs[:2] if merged else outs[3:]
    blocks = columns // PATCH
    inside = blocks - 2
    _, has_before = working(count)

    def lanes(block):
        return slice(block * PATCH, (block + 1) * PATCH)

    upwards = [
        (tile.at[:height, lanes(0)], up[0]),
        (tile.at[:height, PATCH : PATCH * (blocks - 1)], up[1]),
        (tile.at[:height, lanes(blocks - 1)], up[2]),
    ]
    early, late = down
    tall = height - lower
    downwards = [(tile.at[:STRIDE, lanes(b)], early.at[b * STRIDE : (b + 1) * STRIDE, :]) for b in range(blocks)]
    downwards.append((tile.at[first_lower:, : inside * PATCH], late.at[:lower, :]))
    for k in range(2):
        source = lanes(inside + k)
        downwards.append((tile.at[first_lower : first_lower + tall, source], late.at[lower:, lanes(k)]))
        at = lower + k * (lower - tall)
        downwards.append((tile.at[first_lower + tall :, source], late.at[at : at + lower - tall, lanes(2)]))
    peaks_at = lower + 2 * (lower - tall)

    def add_peaks():
        packed[...] = jnp.zeros_like(packed)
        for i in range(patch_rows - upper_rows):
            packed[2 * i : 2 * i + 2, : peaks.shape[2]] = numbers[upper_rows + i].astype(F32)
        late[peaks_at : peaks_at + SLOT, lanes(2)] = packed[...].astype(BF16)

    fixed = [
        (peaks, numbers),
        (tile.at[first_lower:, :PATCH], side),
        (tile.at[:STRIDE, :], top),
        (tile.at[:, :PATCH], left),
    ]
    groups = []
    used = 0
    for group in (upwards, downwards, fixed):
        groups.append([pltpu.make_async_copy(a, b, sems.at[used + k]) for k, (a, b) in enumerate(group)])
        used += len(group)
    upwards, downwards, fixed = groups
    if merged:
        pl.when(has_before)(lambda: start_all(upwards))
        pl.when(jnp.logical_not(has_before))(lambda: start_all(downwards))
        start_all(fixed)
        fixed[0].wait()
        pl.when(jnp.logical_not(has_before))(add_peaks)
        pl.when(has_before)(lambda: wait_all(upwards))
        pl.when(jnp.logical_not(has_before))(lambda: wait_all(downwards))
        wait_all(fixed[1:])
    else:
        start_all(fixed + upwards + downwards)
        fixed[0].wait()
        add_peaks()
        wait_all(fixed[1:] + upwards + downwards)


def own_inner_kernel(
    upper_rows, left_pairs, count, source, tables_source, spectra, tile, constants, energy, sums, once, sems
):
    rows, columns = tile.shape
    patch_rows = rows // STRIDE
    blocks = columns // PATCH
    table = Tables(constants, blocks)

    def chunk(row, block):
        return tile[row * STRIDE : (row + 1) * STRIDE, block * PATCH : (block + 1) * PATCH]

    copies = [
        pltpu.make_async_copy(source, tile, sems.at[0]),
        pltpu.make_async_copy(tables_source, constants, sems.at[1]),
    ]
    start_all(copies)
    wait_all(copies)
    active = working(count)
    inner = 2 * (blocks - 1) * PATCH
    for slot, (lowest, highest) in enumerate(((0, upper_rows), (upper_rows, patch_rows - 2))):

        @pl.when(active[slot])
        def _(slot=slot, lowest=lowest, highest=highest):
            for step in range(lowest // 2, highest // 2):
                columns_of = once.at[step % 2]
                forward(chunk, 2 * step, table, columns_of, range(blocks - 1))
                depth = columns_of.shape[0]
                for part in parts(inner) + [slice(depth - 2 * SLOT, depth)]:
                    value = jnp.dot(columns_of[part, :], table.second(), preferred_element_type=F32)
                    spectra[step, part, :] = value.astype(BF16)
            if slot == 0:
                energy[0, :upper_rows, :] = energies(
                    chunk, range(left_pairs + 1), 0, upper_rows, table.mask(), sums
                )


def own_below_kernel(
    count, tile, below, constants, started, spectra, once
):
    rows, columns = tile.shape
    patch_rows = rows // STRIDE
    blocks = columns // PATCH
    table = Tables(constants, blocks)

    def chunk(row, block):
        lanes = slice(block * PATCH, (block + 1) * PATCH)
        return tile[row * STRIDE : (row + 1) * STRIDE, lanes] if row < patch_rows else below[:, lanes]

    inner = 2 * (blocks - 1) * PATCH
    step = patch_rows // 2 - 1

    @pl.when(working(count)[1])
    def _():
        columns_of = once
        forward(chunk, 2 * step, table, columns_of, range(blocks - 1))
        depth = columns_of.shape[0]
        for part in parts(inner) + [slice(depth - 2 * SLOT, depth)]:
            value = jnp.dot(columns_of[part, :], table.second(), preferred_element_type=F32)
            spectra[step, part, :] = value.astype(BF16)


def own_rest_kernel(
    upper_rows, left_pairs, count, tile, below, beside, corners, constants, started, after_upper, spectra, energy,
    strip, sums, once
):
    rows, columns = tile.shape
    patch_rows = rows // STRIDE
    blocks = columns // PATCH
    table = Tables(constants, blocks)
    strip[:rows, :] = only_low(beside[...])
    strip[rows:, :] = only_low(corners[...])
    active = working(count)

    def chunk(row, block):
        at = slice(row * STRIDE, (row + 1) * STRIDE)
        if block == blocks:
            return strip[at, :]
        lanes = slice(block * PATCH, (block + 1) * PATCH)
        return tile[at, lanes] if row < patch_rows else below[:, lanes]

    inner = 2 * (blocks - 1) * PATCH
    for slot, (lowest, highest) in enumerate(((0, upper_rows), (upper_rows, patch_rows))):

        @pl.when(active[slot])
        def _(slot=slot, lowest=lowest, highest=highest):
            for step in range(lowest // 2, highest // 2):
                columns_of = once.at[step % 2]
                depth = columns_of.shape[0]
                forward(chunk, 2 * step, table, columns_of, [blocks - 1])
                for part in parts(depth, inner):
                    value = jnp.dot(columns_of[part, :], table.second(), preferred_element_type=F32)
                    middle = max(part.start, depth - 2 * SLOT)
                    if part.stop <= middle:
                        spectra[step, part, :] = value.astype(BF16)
                    else:
                        size = part.stop - middle
                        spectra[step, part.start : middle, :] = value[:-size].astype(BF16)
                        before = spectra[step, middle : part.stop, :].astype(F32)
                        spectra[step, middle : part.stop, :] = (before + value[-size:]).astype(BF16)
            energy[slot, : highest - lowest, :] = energies(
                chunk, range(0 if slot else left_pairs, blocks + 1), lowest, highest - lowest, table.mask(), sums
            )


def crossed(own, other, flipped):
    own = own.astype(F32)
    own_re, own_im = own[:, :PATCH], own[:, PATCH:]
    re, im = other[:, :PATCH], other[:, PATCH:]
    real = own_re * re + own_im * im
    imaginary = own_im * re - own_re * im if flipped else own_re * im - own_im * re
    return jnp.concatenate([real.astype(BF16), imaginary.astype(BF16)], 1)


def pair_kernel(
    slot, chosen, first_row, patch_rows, patch_columns, count, peaks_source, early, late, last, beside, left, spectra,
    energy, constants, out, peaks, sem, strip, sums, once, crosses, inverse, peak, moments, offsets, *surfaces
):
    flipped = slot == 1
    size = patch_rows * SLOT
    pairs = patch_columns // 2
    blocks = pairs
    table = Tables(constants, pairs)
    active = working(count)[slot]
    patches = range(2 * chosen[0], 2 * chosen[-1] + 2)

    @pl.when(jnp.logical_not(active))
    def _():
        out[...] = jnp.zeros_like(out)

    @pl.when(active)
    def _():
        fetch = pltpu.make_async_copy(peaks_source.at[:patch_rows], peaks, sem)
        fetch.start()
        if chosen[-1] == pairs - 1:
            if flipped:
                most = patch_rows * STRIDE
                strip[:most, :] = only_low(last[...])
                packed = beside[...].astype(F32)
                strip[most:, :] = only_low(pltpu.roll(packed, STRIDE, 1))
            else:
                packed = beside[: strip.shape[0], :].astype(F32)
                strip[...] = only_low(pltpu.roll(packed, STRIDE, 1))

        def lanes_of(block):
            return slice(block * PATCH, (block + 1) * PATCH)

        def chunk(row, block):
            at = slice(row * STRIDE, (row + 1) * STRIDE)
            if block == blocks:
                return strip[at, :]
            if not flipped:
                if block == 0:
                    return early[at, :]
                return last[at, :] if block == blocks - 1 else late[at, lanes_of(block - 1)]
            if row == patch_rows:
                return early[block * STRIDE : (block + 1) * STRIDE, :]
            inside = blocks - 2
            if block < inside:
                return late[at, lanes_of(block)]
            lower = patch_rows * STRIDE
            tall = late.shape[0] - lower
            start = row * STRIDE
            if start < tall:
                return late[lower + start : lower + start + STRIDE, lanes_of(block - inside)]
            start += lower + (block - inside) * (lower - tall) - tall
            return late[start : start + STRIDE, lanes_of(2)]

        row_of = lax.broadcasted_iota(jnp.int32, (SLOT, 2 * PATCH), 0)
        for step in range(patch_rows // 2):
            columns_of, cross, back = once.at[step % 2], crosses.at[step % 2], inverse.at[step % 2]
            forward(chunk, 2 * step, table, columns_of, chosen)
            depth = columns_of.shape[0]
            if len(chosen) == pairs:
                rows = parts(depth)
            else:
                rows = parts(patches.stop * PATCH, patches.start * PATCH) + [slice(depth - 2 * SLOT, depth)]
            for part in rows:
                spectrum = jnp.dot(columns_of[part, :], table.second(), preferred_element_type=F32)
                cross[part, :] = crossed(spectra[step + first_row // 2, part, :], spectrum, flipped)
            for part in rows:
                back[part, :] = jnp.dot(cross[part, :], table.third(), preferred_element_type=F32).astype(BF16)
            top = 2 * pairs * PATCH
            mid = back[top : top + 2 * SLOT, :PATCH].astype(F32)
            mid = jnp.concatenate([mid[:SLOT], mid[SLOT:]], 1)
            if step == 0:
                fetch.wait()
            for column in patches:
                a = (column // 2) * 2 * PATCH + (column % 2) * HALF
                b = a + PATCH
                right = jnp.concatenate(
                    [
                        jnp.concatenate([back[a : a + HALF, :PATCH], back[b : b + HALF, :PATCH]], 1),
                        jnp.concatenate([back[a : a + HALF, PATCH:], back[b : b + HALF, PATCH:]], 1),
                        jnp.where(row_of == column, mid, 0.0).astype(BF16),
                    ],
                    0,
                )
                value = jnp.dot(table.fourth(), right, preferred_element_type=F32)
                largest = jnp.max(jnp.abs(value), axis=0, keepdims=True)
                for which in range(2):
                    lanes = slice(which * PATCH, (which + 1) * PATCH)
                    i = 2 * step + which
                    at = i * SLOT + column
                    surface = surfaces[2 * (column - patches.start) + which]
                    surface[EDGE : EDGE + PATCH, :] = value[:, lanes]
                    surface[:EDGE, :] = value[PATCH - EDGE :, lanes]
                    surface[EDGE + PATCH :, :] = value[:EDGE, lanes]
                    peak[at : at + 1, :] = largest[:, lanes]
                    along = peaks[i, 1, column] + (EDGE - WIN // 2)
                    moments[at * 8 : at * 8 + 8, :] = surface[pl.ds(along, 8), :]
                    offsets[at : at + 1, :] = jnp.full((1, PATCH), peaks[i, 0, column], jnp.int32)
        other = energies(chunk, range(chosen[0], chosen[-1] + 2), 0, patch_rows, table.mask(), sums)
        scales = float(PATCH) ** 3 * jnp.sqrt((energy[slot, :patch_rows, :] + 1e-05) * (other + 1e-05))

        lane = lax.broadcasted_iota(jnp.int32, (1, PATCH), 1)
        scale = jnp.ones((1, PATCH), F32)
        for i in range(patch_rows):
            row = scales[i : i + 1, :]
            row = pltpu.roll(row, i * SLOT, 1) if i else row
            scale = jnp.where((lane >= i * SLOT + patches.start) & (lane < i * SLOT + patches.stop), row, scale)
        peak_rows = peak[...]
        height = jnp.max(jnp.transpose(peak_rows), axis=0, keepdims=True) / scale + 1e-05

        lane = lax.broadcasted_iota(jnp.int32, (size, PATCH), 1)
        offset = (lane - offsets[...] + (WIN // 2 + PATCH)) & (PATCH - 1)
        u = (offset - WIN // 2).astype(F32)
        within = offset < WIN
        numbers = np.arange(WIN) - WIN // 2
        middle_square = float(np.mean(numbers**2))
        u0 = jnp.where(within, 1.0, 0.0)
        u1 = jnp.where(within, u, 0.0)
        u2 = jnp.where(within, u * u - middle_square, 0.0)
        v0 = v1 = v2 = jnp.zeros((size, PATCH), F32)
        for v in range(WIN):
            value = moments[pl.ds(v, size, stride=8), :]
            position = float(v - WIN // 2)
            v0 += value
            v1 += position * value
            v2 += (position * position - middle_square) * value
        factors = ((u0, v0), (u1, v0), (u0, v1), (u2, v0), (u0, v2), (u1, v1))
        terms = [two_terms(fu * fv) for fu, fv in factors]
        which_e = lax.broadcasted_iota(jnp.int32, (SLOT, len(terms) * PATCH), 0)
        of_lane = lax.broadcasted_iota(jnp.int32, (SLOT, len(terms) * PATCH), 1)
        ones = jnp.where((of_lane >= which_e * PATCH) & (of_lane < (which_e + 1) * PATCH), 1.0, 0.0).astype(BF16)
        total = sum(
            lax.dot_general(
                ones, jnp.concatenate([t[k] for t in terms], 1), (((1,), (1,)), ((), ())), preferred_element_type=F32
            )
            for k in range(2)
        )[:8]
        linear = float(np.sum(numbers**2))
        quadratic = float(np.sum((numbers**2 - middle_square) ** 2))
        norms = (
            float(WIN), math.sqrt(WIN * linear), math.sqrt(WIN * linear), math.sqrt(WIN * quadratic),
            math.sqrt(WIN * quadratic), linear,
        )
        e_row = lax.broadcasted_iota(jnp.int32, (8, size), 0)
        factor = jnp.zeros((8, size), F32)
        for e, norm in enumerate(norms):
            factor = jnp.where(e_row == e, 1.0 / norm, factor)
        result = total * factor / (scale * height)[:, :size]
        if chosen[0] > 0:
            slot_lane = lax.broadcasted_iota(jnp.int32, (8, size), 1) & (SLOT - 1)
            result = jnp.where(slot_lane < patches.start, left[:, :size], result)
        out[:, :size] = result
        if size < PATCH:
            out[:, size:] = jnp.zeros((8, PATCH - size), F32)


def join_kernel(upper_rows, upper, lower, valid, out):
    count, patch_rows, _, patch_columns = out.shape
    for i in range(patch_rows):
        source, at = (upper, i) if i < upper_rows else (lower, i - upper_rows)
        value = source[...]
        turned = pltpu.roll(value, PATCH - at * SLOT, 1) if at else value
        keep = valid[i].astype(F32)
        for e in range(count):
            out[e, i] = turned[e : e + 1, :patch_columns] * keep


def body(sections, peaks, valid):
    tile = sections[0]
    rows, columns = tile.shape
    patch_rows, patch_columns = rows // STRIDE, columns // STRIDE
    pairs = patch_columns // 2
    upper_rows = (patch_rows // 2 + 1) // 2 * 2
    lower_rows = patch_rows - upper_rows
    first_lower = upper_rows * STRIDE
    upper_height = first_lower + STRIDE
    lower_height = lower_rows * STRIDE + STRIDE
    count, height = lax.axis_size("gz"), lax.axis_size("gy")
    peaks = jnp.transpose(peaks, (0, 2, 1, 3))[0]
    valid = jnp.transpose(valid, (1, 0, 2))

    constants = jnp.asarray(all_tables(columns // PATCH + 1, patch_columns), BF16)

    vmem = pl.BlockSpec(memory_space=pltpu.VMEM)

    def grant(mib):
        return pltpu.CompilerParams(vmem_limit_bytes=mib << 20)

    def shape(*dims, dtype=BF16):
        return jax.ShapeDtypeStruct(dims, dtype)

    merged = count == 2
    early, late, last = shape(upper_height, PATCH), shape(upper_height, columns - 2 * PATCH), shape(upper_height, PATCH)
    hbm = pl.BlockSpec(memory_space=pltpu.HBM)

    def held(value):
        return pltpu.with_memory_space_constraint(value, pltpu.HBM)

    copies = 3 + columns // PATCH + 5 + 4
    outs = pl.pallas_call(
        functools.partial(prepare_kernel, upper_rows, merged, count),
        out_shape=((early, late, last) if merged else (early, late, last, early, late))
        + (shape(rows - first_lower, PATCH), shape(STRIDE, columns), shape(rows, PATCH)),
        in_specs=[hbm] * 2,
        out_specs=(vmem,) * (6 if merged else 8),
        scratch_shapes=[
            pltpu.VMEM(peaks.shape, jnp.int32),
            pltpu.VMEM((SLOT, PATCH), F32),
            pltpu.SemaphoreType.DMA((copies,)),
        ],
        compiler_params=grant(1),
        name="prepare",
    )(held(tile), held(peaks))
    side, top, left = outs[-3:]

    up = [((s + 1) * height + y, s * height + y) for s in range(count - 1) for y in range(height)]
    down = [(s * height + y + 1, (s + 1) * height + y) for s in range(count - 1) for y in range(height - 1)]
    across = lax.axis_size("gx")
    slant = [(s * across + x + 1, (s + 1) * across + x) for s in range(count - 1) for x in range(across - 1)]
    side = lax.ppermute(side, ("gz", "gx"), slant)
    if merged:
        early_upper = early_lower = lax.ppermute(outs[0], ("gz", "gy"), up + down)
        late_upper = late_lower = lax.ppermute(outs[1], "gz", [(0, 1), (1, 0)])
    else:
        early_upper = lax.ppermute(outs[0], ("gz", "gy"), up)
        early_lower = lax.ppermute(outs[3], ("gz", "gy"), down)
        late_upper = passed_along(outs[1], "gz", -1)
        late_lower = passed_along(outs[4], "gz", 1)
    last_upper = passed_along(outs[2], "gz", -1)
    steps_up = [(s * height + y + 1, s * height + y) for s in range(1, count) for y in range(height - 1)]
    below = lax.ppermute(top, ("gz", "gy"), steps_up)
    others = jnp.pad(early_upper[:, :STRIDE], ((0, rows - upper_height), (0, 0)))
    beside = passed_along(jnp.concatenate([left[:, :STRIDE], others], 1), "gx", -1)
    corners = jnp.concatenate([below[:, :STRIDE], early_lower[:STRIDE, :STRIDE]], 1)
    level = [(s * across + x + 1, s * across + x) for s in range(1, count) for x in range(across - 1)]
    corners = lax.ppermute(corners, ("gz", "gx"), level)

    steps = patch_rows // 2
    depth = 2 * pairs * PATCH + 2 * SLOT
    width = columns + PATCH
    split = pairs - 2
    own_cost = pl.CostEstimate(flops=2_000_000_000, bytes_accessed=6_000_000, transcendentals=0)
    own_inner = pl.pallas_call(
        functools.partial(own_inner_kernel, upper_rows, split, count),
        out_shape=(
            shape(steps, depth, 2 * PATCH), shape(rows, columns), shape(*constants.shape), shape(2, 8, PATCH, dtype=F32)
        ),
        in_specs=[hbm] * 2,
        out_specs=(vmem,) * 4,
        scratch_shapes=[pltpu.VMEM((8, width), F32), pltpu.VMEM((2, depth, 2 * PATCH), BF16), pltpu.SemaphoreType.DMA((2,))],
        compiler_params=grant(6),
        cost_estimate=own_cost,
        name="own_inner",
    )
    spectra, tile, constants, energy_left = own_inner(held(tile), held(constants))

    def correlated(slot, chosen, first_row, count_rows, strip_rows, peaks_here, spectra, energy, *pieces):
        size = count_rows * SLOT
        return pl.pallas_call(
            functools.partial(pair_kernel, slot, chosen, first_row, count_rows, patch_columns, count),
            out_shape=shape(8, PATCH, dtype=F32),
            in_specs=[pl.BlockSpec(memory_space=pl.ANY)] + [vmem] * 8,
            out_specs=vmem,
            scratch_shapes=[
                pltpu.SMEM((count_rows, 2, patch_columns), jnp.int32),
                pltpu.SemaphoreType.DMA,
                pltpu.VMEM((strip_rows, PATCH), BF16),
                pltpu.VMEM((8, width), F32),
                pltpu.VMEM((2, depth, 2 * PATCH), BF16),
                pltpu.VMEM((2, depth, 2 * PATCH), BF16),
                pltpu.VMEM((2, depth, 2 * PATCH), BF16),
                pltpu.VMEM((PATCH, PATCH), F32),
                pltpu.VMEM((size * 8, PATCH), F32),
                pltpu.VMEM((size, PATCH), jnp.int32),
            ]
            + [pltpu.VMEM((PATCH + 2 * EDGE, PATCH), F32)] * (4 * len(chosen)),
            compiler_params=grant(12),
            cost_estimate=pl.CostEstimate(flops=4_000_000_000, bytes_accessed=6_000_000, transcendentals=0),
        )(peaks_here, *pieces, spectra, energy, constants)

    own_below = pl.pallas_call(
        functools.partial(own_below_kernel, count),
        out_shape=shape(steps, depth, 2 * PATCH),
        in_specs=[vmem] * 4,
        out_specs=vmem,
        scratch_shapes=[pltpu.VMEM((depth, 2 * PATCH), BF16)],
        input_output_aliases={3: 0},
        compiler_params=grant(4),
        cost_estimate=own_cost,
        name="own_below",
    )
    spectra = own_below(tile, below, constants, spectra)
    at = lower_rows * STRIDE + 2 * (2 * lower_rows * STRIDE - upper_height)
    lanes = 2 * PATCH
    peaks_lower = late_lower[at : at + 2 * lower_rows, lanes : lanes + patch_columns].astype(jnp.int32)
    peaks_lower = peaks_lower.reshape(lower_rows, 2, patch_columns)
    upper_part = (0, upper_rows, upper_height, peaks)
    lower_part = (upper_rows, lower_rows, lower_height, peaks_lower)
    nothing = energy_left[0]
    upper_left = correlated(
        0, range(split), *upper_part, spectra, energy_left, early_upper, late_upper, nothing, nothing, nothing
    )
    own_rest = pl.pallas_call(
        functools.partial(own_rest_kernel, upper_rows, split, count),
        out_shape=(shape(steps, depth, 2 * PATCH), shape(2, 8, PATCH, dtype=F32)),
        in_specs=[vmem] * 7,
        out_specs=(vmem, vmem),
        scratch_shapes=[
            pltpu.VMEM((rows + STRIDE, PATCH), BF16),
            pltpu.VMEM((8, width), F32),
            pltpu.VMEM((2, depth, 2 * PATCH), BF16),
        ],
        input_output_aliases={5: 0},
        compiler_params=grant(6),
        cost_estimate=own_cost,
        name="own_rest",
    )
    spectra, energy = own_rest(tile, below, beside, corners, constants, spectra, upper_left)

    rest = range(split, pairs)
    lower = correlated(1, range(pairs), *lower_part, spectra, energy, early_lower, late_lower, side, corners, nothing)
    lower = passed_along(lower, "gz", -1)
    upper = correlated(0, rest, *upper_part, spectra, energy, early_upper, late_upper, last_upper, beside, upper_left)
    fit = pl.pallas_call(
        functools.partial(join_kernel, upper_rows),
        out_shape=shape(6, patch_rows, 1, patch_columns, dtype=F32),
        in_specs=[vmem] * 3,
        out_specs=vmem,
        compiler_params=grant(1),
        name="join",
    )(upper, lower, valid)
    return jnp.transpose(fit, (2, 0, 1, 3))


def solution(mesh):
    in_specs = (P("gz", "gy", "gx"), P("gz", None, "gy", "gx"), P("gz", "gy", "gx"))
    out_specs = P("gz", None, "gy", "gx")
    return jax.shard_map(body, mesh=mesh, in_specs=in_specs, out_specs=out_specs, check_vma=False)
```
